256 devices in a mesh: seq: 64 (over x, z, core), exp: 4 (over y).
Axes of the slice: x: 4, y: 4, z: 8, core: 2. Of those that a mesh axis runs over, the one named last changes fastest.
Arguments:
- residual: bfloat16 [8192, 2048], P('seq', 'exp'), may hold values from -36 to 36
- queries: bfloat16 [8192, 2048], P('seq', 'exp'), may hold values from -6 to 6
- key_vectors: bfloat16 [8192, 2048], P('seq', 'exp'), may hold values from -6 to 6
- value_vectors: bfloat16 [8192, 2048], P('seq', 'exp'), may hold values from -36 to 36
- head_gain: float32 [2048], P('exp'), may hold values from 0.25 to 1.75
- norm_gain: float32 [2048], replicated, may hold values from 0.25 to 1.75
- routes: int32 [8192, 8], P('seq'), may hold values from 0 to 63, as said below
- route_gates: float32 [8192, 8], P('seq'), may hold values from 0.2 to 1
- expert_in: bfloat16 [64, 2, 2048, 1024], P('seq'), may hold values from -0.125 to 0.125
- expert_out: bfloat16 [64, 1024, 2048], P('seq'), may hold values from -0.1875 to 0.1875
Outputs:
- layer_out: bfloat16 [8192, 2048], P('seq', 'exp')
The draws below stay inside these ranges and needn't reach their ends.
Inputs may be any that keep to these rules, and one draw needn't show every extreme that they name: `routes`: each row names 8 different experts. In every aligned block of 32 rows no expert is named by more than 6 rows, and the same 10 experts are named by exactly 6 rows in every block.
All inputs are finite; a program needn't handle non-finite values.
Results may differ from the reference program's by a relative error of at most 0.0075.
Values may be sent and summed in bfloat16 or wider, within the bound.
A program may use at most 128 MiB of HBM per device.

```python
import math
import jax
import jax.numpy as jnp
from jax import lax

D = 2048
HEADS = 16
HEAD = 128
FF = 1024
TOPK = 8
EXPERTS = 64
TOK_DEV = 128
SEQ_LEN = 8192
SUB = 32
CAP = 6
HOT = 10


def draw_residual(key, part):
    key_base, key_cols, key_rows = jax.random.split(jax.random.fold_in(key, 5), 3)
    entries = jnp.clip(jax.random.normal(key_base, (SEQ_LEN, D), jnp.float32), -6.0, 6.0)
    column_scale = jnp.exp(jax.random.uniform(key_cols, (D,), jnp.float32, math.log(0.3), math.log(3.0)))
    row_scale = jnp.exp(jax.random.uniform(key_rows, (SEQ_LEN, 1), jnp.float32, math.log(0.5), math.log(2.0)))
    return (entries * column_scale[None, :] * row_scale).astype(jnp.bfloat16)


def draw_value_vectors(key, part):
    key_base, key_cols, key_rows = jax.random.split(jax.random.fold_in(key, 9), 3)
    entries = jnp.clip(jax.random.normal(key_base, (SEQ_LEN, D), jnp.float32), -6.0, 6.0)
    column_scale = jnp.exp(jax.random.uniform(key_cols, (D,), jnp.float32, math.log(0.3), math.log(3.0)))
    row_scale = jnp.exp(jax.random.uniform(key_rows, (SEQ_LEN, 1), jnp.float32, math.log(0.5), math.log(2.0)))
    return (entries * column_scale[None, :] * row_scale).astype(jnp.bfloat16)


def draw_routes(key, part):
    key_order, key_blocks = jax.random.split(jax.random.fold_in(key, 17), 2)
    expert_order = jax.random.permutation(key_order, EXPERTS).astype(jnp.int32)
    per_block = SUB * TOPK
    remainder = per_block - HOT * CAP
    cold_count = EXPERTS - HOT
    base_load = remainder // cold_count
    extra_count = remainder - base_load * cold_count
    spread = max(0, min(base_load, CAP - base_load - 1))
    pair_count = cold_count // 2
    block_count = SEQ_LEN // SUB
    positions = jnp.arange(per_block, dtype=jnp.int32)
    hot_loads = jnp.full((HOT,), CAP, jnp.int32)

    def one_block(block_key):
        key_pick, key_pair, key_shift, key_rows, key_cols = jax.random.split(block_key, 5)
        ranking = jax.random.permutation(key_pick, cold_count)
        load_counts = base_load + (ranking < extra_count).astype(jnp.int32)
        pairing = jax.random.permutation(key_pair, cold_count)
        shifts = jax.random.randint(key_shift, (pair_count,), 0, spread + 1, dtype=jnp.int32)
        load_counts = load_counts.at[pairing[0:2 * pair_count:2]].add(-shifts)
        load_counts = load_counts.at[pairing[1:2 * pair_count:2]].add(shifts)
        segment_ends = jnp.cumsum(jnp.concatenate([hot_loads, load_counts]))
        segment = jnp.sum((positions[:, None] >= segment_ends[None, :]).astype(jnp.int32), axis=1)
        chosen = expert_order[segment].reshape(TOPK, SUB).T
        row_order = jax.random.permutation(key_rows, SUB)
        column_order = jax.random.permutation(key_cols, TOPK)
        return chosen[row_order][:, column_order]
    block_keys = jax.random.split(key_blocks, block_count)
    return jax.vmap(one_block)(block_keys).reshape(SEQ_LEN, TOPK).astype(jnp.int32)


def levels(stream_key, extent, cuts, low, high):
    gain = 1.0
    for dim, parts in cuts:
        heights = jax.random.uniform(jax.random.fold_in(jax.random.fold_in(stream_key, 6), dim), (parts,), jnp.float32, low / len(cuts), high / len(cuts))
        gain = gain * jnp.repeat(jnp.exp(heights), extent[dim] // parts).reshape((-1,) + (1,) * (len(extent) - 1 - dim))
    return gain


def bell_draw(stream_key, dims, scale, limit, shards=(), held_as=jnp.bfloat16):
    gain = levels(stream_key, dims, shards, -0.22, 0.18) if shards else 1.0
    values = jax.random.normal(stream_key, dims, jnp.float32) * scale * gain
    return jnp.minimum(jnp.maximum(values, -limit), limit).astype(held_as)


def setup_inputs(seed: int = 0) -> dict:
    key_list = jax.random.split(jax.random.key(seed), 11)
    residual = draw_residual(jax.random.fold_in(key_list[10], 71), 0)
    queries = bell_draw(key_list[1], (SEQ_LEN, D), 1.0, 6.0, ((0, 64), (1, 4)))
    key_vectors = bell_draw(key_list[2], (SEQ_LEN, D), 1.0, 6.0, ((0, 64), (1, 4)))
    value_vectors = draw_value_vectors(jax.random.fold_in(key_list[10], 71), 0)
    head_gain = jnp.clip(1.0 + 0.15 * jax.random.normal(key_list[4], (D,), jnp.float32), 0.25, 1.75)
    norm_gain = jnp.clip(1.0 + 0.15 * jax.random.normal(key_list[5], (D,), jnp.float32), 0.25, 1.75)
    routes = draw_routes(jax.random.fold_in(key_list[10], 71), 0)
    route_gates = jnp.clip(0.2 + 0.8 * jax.random.uniform(key_list[7], (SEQ_LEN, TOPK), jnp.float32) ** levels(key_list[7], (SEQ_LEN, TOPK), ((0, 64),), -0.2, 0.2), 0.2, 1.0)
    expert_in = bell_draw(key_list[8], (EXPERTS, 2, D, FF), D ** -0.5, 0.125, ((0, 64),))
    expert_out = bell_draw(key_list[9], (EXPERTS, FF, D), FF ** -0.5, 0.1875, ((0, 64),))
    return dict(residual=residual, queries=queries, key_vectors=key_vectors, value_vectors=value_vectors, head_gain=head_gain, norm_gain=norm_gain, routes=routes, route_gates=route_gates, expert_in=expert_in, expert_out=expert_out)


def to_blocks(matrix):
    return matrix.astype(jnp.float32).reshape(matrix.shape[0] // TOK_DEV, TOK_DEV, HEADS, HEAD)

def attend_block(state_sum, block_triple):
    query_block, key_block, value_block = block_triple
    causal = jnp.tril(jnp.ones((TOK_DEV, TOK_DEV), jnp.float32))
    carried = jnp.einsum('bhd,hde->bhe', query_block, state_sum, precision=lax.Precision.HIGHEST)
    scores = jnp.einsum('bhd,chd->hbc', query_block, key_block, precision=lax.Precision.HIGHEST) * causal[None]
    within = jnp.einsum('hbc,che->bhe', scores, value_block, precision=lax.Precision.HIGHEST)
    state_sum = state_sum + jnp.einsum('chd,che->hde', key_block, value_block, precision=lax.Precision.HIGHEST)
    return (state_sum, carried + within)

def mix_experts(normed, routes, route_gates, expert_in, expert_out):
    length = normed.shape[0]
    block_rows = 256
    flat_routes = routes.reshape(-1).astype(jnp.int32)
    route_total = flat_routes.shape[0]
    expert_ids = jnp.arange(EXPERTS, dtype=jnp.int32)
    counts = lax.optimization_barrier(jnp.sum((flat_routes[:, None] == expert_ids[None, :]).astype(jnp.int32), axis=0))
    starts = jnp.cumsum(counts) - counts
    padded = (counts + block_rows - 1) // block_rows * block_rows
    padded_starts = jnp.cumsum(padded) - padded
    route_order = jnp.argsort(flat_routes, stable=True).astype(jnp.int32)
    flat_gates = route_gates.reshape(-1)
    block_count = (route_total + block_rows - 1) // block_rows + EXPERTS
    offsets = jnp.arange(block_rows, dtype=jnp.int32)

    def one_block(running, block_index):
        first_row = block_index * block_rows
        expert = jnp.minimum(jnp.sum((padded_starts + padded <= first_row).astype(jnp.int32)), EXPERTS - 1)
        within = first_row - padded_starts[expert] + offsets
        live_rows = (within >= 0) & (within < counts[expert])
        position = jnp.clip(starts[expert] + within, 0, route_total - 1).astype(jnp.int32)
        route_index = route_order[position]
        token_index = (route_index // TOPK).astype(jnp.int32)
        weight = jnp.where(live_rows, flat_gates[route_index], jnp.zeros((), flat_gates.dtype))
        chosen = normed[token_index]
        pair_weights = expert_in[expert]
        gate_pre = jnp.dot(chosen, pair_weights[0], preferred_element_type=jnp.float32)
        up_pre = jnp.dot(chosen, pair_weights[1], preferred_element_type=jnp.float32)
        activated = (jax.nn.silu(gate_pre) * up_pre).astype(jnp.bfloat16)
        produced = jnp.dot(activated, expert_out[expert], preferred_element_type=jnp.float32).astype(jnp.bfloat16)
        produced = lax.optimization_barrier(produced).astype(jnp.float32)
        running = running.at[token_index].add(weight[:, None] * produced)
        return (running, None)
    zero_sum = jnp.zeros((length, D), jnp.float32)
    result, unused = lax.scan(one_block, zero_sum, jnp.arange(block_count, dtype=jnp.int32))
    return result

def reference(residual, queries, key_vectors, value_vectors, head_gain, norm_gain, routes, route_gates, expert_in, expert_out):
    length = residual.shape[0]
    initial = jnp.zeros((HEADS, HEAD, HEAD), jnp.float32)
    final_state, outputs = lax.scan(attend_block, initial, (to_blocks(queries), to_blocks(key_vectors), to_blocks(value_vectors)))
    raw_output = outputs.reshape(length, HEADS, HEAD)
    scaled = raw_output * lax.rsqrt(lax.optimization_barrier(jnp.mean(raw_output * raw_output, axis=-1, keepdims=True)) + 1e-06)
    attention_out = scaled.reshape(length, D) * head_gain
    hidden = (residual.astype(jnp.float32) + attention_out).astype(jnp.bfloat16)
    widened = hidden.astype(jnp.float32)
    normed = (widened * lax.rsqrt(lax.optimization_barrier(jnp.mean(widened * widened, axis=-1, keepdims=True)) + 1e-06) * norm_gain).astype(jnp.bfloat16)
    moe_out = mix_experts(normed, routes, route_gates, expert_in, expert_out)
    return (widened + moe_out).astype(jnp.bfloat16)
```

```python
import functools

import jax
import jax.numpy as jnp
from jax import lax
from jax.experimental import pallas as pl
from jax.experimental.pallas import tpu as pltpu
from jax.sharding import PartitionSpec as P

MESH = pl.DeviceIdType.MESH
F32 = jnp.float32
BF16 = jnp.bfloat16

HEAD = 128
XS, ZS, CS, YS = 4, 8, 2, 4
SEQ = XS * ZS * CS
D = 2048
FF = 1024
SUB = 32
CAP = 6
NC = 4
CW = D // NC
PER_Y = NC // YS
GROUP = ZS * CAP
ROWS = XS * CS * GROUP
TILE = 256
PEERS = ((2, 0), (2, 1), (1, 0), (3, 0), (1, 1), (3, 1), (0, 1))


def nt(a, b):
    return lax.dot_general(a, b, (((1,), (1,)), ((), ())), preferred_element_type=F32)


def tn(a, b):
    return lax.dot_general(a, b, (((0,), (0,)), ((), ())), preferred_element_type=F32)


def nn(a, b):
    return jnp.dot(a, b, preferred_element_type=F32)


def halves(value):
    high = value.astype(BF16)
    return high, (value - high.astype(F32)).astype(BF16)


def layer_kernel(
    q_ref, k_ref, v_ref, res_ref, hgain_ref, ngain_ref, routes_ref, gates_ref, win_ref, wout_ref,
    out_ref,
    w1, w2, state, gathered, running, prior, raw, hidden, rows, meta, place, mixhi, mixlo,
    blk, sel, xin, acc, act, yout, ret, part, rs_send, rs_recv, mine, moe,
    w_sem, st_send, st_recv, pr_send, pr_recv, meta_send, meta_recv, y_send, y_recv,
    ag_send, ag_recv, xs_send, xs_recv, loc_sem, rt_send, rt_recv, rs_ssem, rs_rsem, fy_send, fy_recv,
):
    me = lax.axis_index("seq")
    y = lax.axis_index("exp")
    x = me // (ZS * CS)
    z = (me // CS) % ZS
    c = me % CS
    mine_d = x * CS + c

    def seq_id(xx, zz, cc):
        return (xx * ZS + zz) * CS + cc

    def remote(src, dst, ssem, rsem, seq=None, exp=None):
        return pltpu.make_async_remote_copy(
            src_ref=src, dst_ref=dst, send_sem=ssem, recv_sem=rsem,
            device_id=(me if seq is None else seq, y if exp is None else exp),
            device_id_type=MESH,
        )

    pending = []

    def go(copy):
        copy.start()
        pending.append(copy)
        return copy

    weights = []
    for q in range(NC):
        for g in range(2):
            weights.append(pltpu.make_async_copy(
                win_ref.at[0, g, pl.ds(q * CW, CW), :], w1.at[g, q], w_sem.at[0]))
    for q in range(NC):
        weights.append(pltpu.make_async_copy(
            wout_ref.at[0, :, pl.ds(q * CW, CW)], w2.at[q], w_sem.at[1]))
    for copy in weights:
        copy.start()

    barrier = pltpu.get_barrier_semaphore()

    def greet(i, _):
        pl.semaphore_signal(barrier, inc=1, device_id=((me + i) % SEQ, y), device_id_type=MESH)
        return 0

    lax.fori_loop(1, SEQ, greet, 0)
    for j in range(1, YS):
        pl.semaphore_signal(barrier, inc=1, device_id=(me, (y + j) % YS), device_id_type=MESH)

    heads = q_ref.shape[1] // HEAD
    for h in range(heads):
        cols = pl.ds(h * HEAD, HEAD)
        outer = tn(k_ref[:, cols], v_ref[:, cols])
        state[pl.ds(h * 16, 16)] = outer.reshape(16, 8, HEAD)

    lane = lax.broadcasted_iota(jnp.int32, (SUB, 128), 1)
    my_rows = pl.ds(pl.multiple_of(y * SUB, SUB), SUB)
    my_routes = routes_ref[my_rows, :]
    my_gates = gates_ref[my_rows, :]
    onehot = jnp.zeros((SUB, 128), F32)
    gate_lanes = jnp.zeros((SUB, 128), F32)
    for k in range(my_routes.shape[1]):
        route = my_routes[:, k:k + 1]
        onehot = onehot + jnp.where(route == lane, 1.0, 0.0)
        gate_lanes = gate_lanes + jnp.where(route + 64 == lane, my_gates[:, k:k + 1], 0.0)
    earlier = jnp.where(
        lax.broadcasted_iota(jnp.int32, (SUB, SUB), 0) > lax.broadcasted_iota(jnp.int32, (SUB, SUB), 1),
        1.0, 0.0).astype(BF16)
    rank = nn(earlier, onehot.astype(BF16))
    meta[0] = onehot * (rank + 1.0) + gate_lanes

    pl.semaphore_wait(barrier, SEQ - 1 + YS - 1)

    def send_state(i, _):
        for peer in ((me + i) % SEQ, (me + SEQ - i) % SEQ):
            remote(state.at[peer], gathered.at[me], st_send, st_recv, seq=peer).start()
        return 0

    lax.fori_loop(1, SEQ // 2, send_state, 0)
    far = (me + SEQ // 2) % SEQ
    remote(state.at[far], gathered.at[me], st_send, st_recv, seq=far).start()
    gathered[me] = state[me]

    for k in range(1, ZS):
        go(remote(meta.at[0], meta.at[k], meta_send.at[k - 1], meta_recv.at[k - 1],
                  seq=seq_id(x, (z + k) % ZS, c)))

    causal = (lax.broadcasted_iota(jnp.int32, (128, 128), 0)
              >= lax.broadcasted_iota(jnp.int32, (128, 128), 1))
    for h in range(heads):
        cols = pl.ds(h * HEAD, HEAD)
        scores = jnp.where(causal, nt(q_ref[:, cols], k_ref[:, cols]), 0.0)
        high, low = halves(scores)
        raw[:, cols] = nn(high, v_ref[:, cols]) + nn(low, v_ref[:, cols])

    def others(ref):
        return ref.at[pl.ds(0, SEQ - 1)]

    remote(others(state), others(gathered), st_send, st_recv).wait_recv()

    def scan_step(s, total):
        running[s] = total
        return total + gathered[s]

    lax.fori_loop(0, SEQ, scan_step, jnp.zeros((8, HEAD), F32))

    def send_prior(i, _):
        for peer in ((me + i) % SEQ, (me + SEQ - i) % SEQ):
            remote(running.at[peer], prior.at[me], pr_send, pr_recv, seq=peer).start()
        return 0

    lax.fori_loop(1, SEQ // 2, send_prior, 0)
    remote(running.at[far], prior.at[me], pr_send, pr_recv, seq=far).start()
    prior[me] = running[me]

    for copy in pending[:ZS - 1]:
        copy.wait_recv()
    everyone = meta[...].reshape(ZS * SUB, 128)
    meta_hi, meta_lo = halves(everyone)

    def slot_parts(shape, dim):
        index = lax.broadcasted_iota(jnp.int32, shape, dim)
        group = (index * 10923) >> 16
        return group >> 3, group & 7, index - group * 6

    d_of, k_of, r_of = slot_parts((ROWS, 128), 0)
    expert_of = seq_id(d_of >> 1, z, d_of & 1)
    lanes = lax.broadcasted_iota(jnp.int32, (ROWS, 128), 1)
    pick_rank = jnp.where(lanes == expert_of, 1.0, 0.0).astype(BF16)
    pick_gate = jnp.where(lanes == expert_of + 64, 1.0, 0.0).astype(BF16)
    _, k_row, r_row = slot_parts((ROWS, ZS * SUB), 0)
    k_col = lax.broadcasted_iota(jnp.int32, (ROWS, ZS * SUB), 1) >> 5
    found = (nt(pick_rank, meta_hi) == (r_row + 1).astype(F32)) & (k_row == k_col)
    place[...] = jnp.where(found, 1.0, 0.0).astype(BF16)
    _, k_row, r_row = slot_parts((ZS * SUB, ROWS), 1)
    k_col = lax.broadcasted_iota(jnp.int32, (ZS * SUB, ROWS), 0) >> 5
    found = (nt(meta_hi, pick_rank) == (r_row + 1).astype(F32)) & (k_row == k_col)
    mix = jnp.where(found, nt(meta_hi, pick_gate) + nt(meta_lo, pick_gate), 0.0)
    high, low = halves(mix)
    mixhi[...] = high
    mixlo[...] = low
    acc[...] = jnp.zeros(acc.shape, F32)

    remote(others(running), others(prior), pr_send, pr_recv).wait_recv()
    for h in range(heads):
        cols = pl.ds(h * HEAD, HEAD)
        high, low = halves(prior[pl.ds(h * 16, 16)].reshape(HEAD, HEAD))
        total = nn(q_ref[:, cols], high) + nn(q_ref[:, cols], low) + raw[:, cols]
        scale = lax.rsqrt(jnp.mean(total * total, axis=1, keepdims=True) + 1e-6)
        hidden[:, cols] = (res_ref[:, cols].astype(F32) + total * scale * hgain_ref[:, cols]).astype(BF16)

    y_copies = []
    for j in range(1, YS):
        peer = (y + j) % YS
        y_copies.append(go(remote(
            hidden.at[pl.ds(pl.multiple_of(peer * SUB, SUB), SUB), :], rows.at[y],
            y_send.at[j - 1], y_recv.at[j - 1], exp=peer)))
    rows[y] = hidden[my_rows, :]
    for copy in y_copies:
        copy.wait_recv()
    wide = [rows[j].astype(F32) for j in range(YS)]
    square = sum(jnp.sum(w * w, axis=1, keepdims=True) for w in wide)
    scale = lax.rsqrt(square * (1.0 / D) + 1e-6)
    for q in range(NC):
        part_cols = wide[q // PER_Y][:, (q % PER_Y) * CW:(q % PER_Y + 1) * CW]
        blk[q, 0] = (part_cols * scale * ngain_ref[:, q * CW:(q + 1) * CW]).astype(BF16)

    right = seq_id(x, (z + 1) % ZS, c)
    left = seq_id(x, (z + ZS - 1) % ZS, c)
    far_k = ZS // 2
    ag = {}

    def ag_right(q, k):
        ag["r", q, k] = go(remote(blk.at[q, k - 1], blk.at[q, k], ag_send.at[q, k - 1],
                                  ag_recv.at[q, k - 1], seq=right))

    def ag_left(q, k):
        ag["l", q, k] = go(remote(blk.at[q, (ZS - k + 1) % ZS], blk.at[q, ZS - k], ag_send.at[q, ZS - k - 1],
                                  ag_recv.at[q, ZS - k - 1], seq=left))

    def ag_step(q, k):
        if k > 0:
            ag["r", q, k].wait_recv()
        if k < far_k:
            ag_right(q, k + 1)
        if 0 < k < far_k:
            ag["l", q, k].wait_recv()
        if k + 1 < far_k:
            ag_left(q, k + 1)

    xs = {}

    def select(q):
        chosen = nn(place[...], blk[q].reshape(ZS * SUB, CW)).astype(BF16)
        sel[q] = chosen.reshape(XS * CS, GROUP, CW)
        for j, (dx, dc) in enumerate(PEERS):
            xx, cc = (x + dx) % XS, (c + dc) % CS
            xs[q, j] = go(remote(sel.at[q, xx * CS + cc], xin.at[q, mine_d], xs_send.at[q, j],
                                 xs_recv.at[q, j], seq=seq_id(xx, z, cc)))
        own = pltpu.make_async_copy(sel.at[q, mine_d], xin.at[q, mine_d], loc_sem.at[0, q])
        own.start()
        xs[q, "own"] = own

    def expert_up(q):
        if q == 0:
            pltpu.make_async_copy(w1, w1, w_sem.at[0]).wait()
        for j in range(len(PEERS)):
            xs[q, j].wait_recv()
        xs[q, "own"].wait()

        def tile(i, _):
            cols = pl.ds(pl.multiple_of((i % 4) * TILE, TILE), TILE)
            acc[i] += nn(xin[q].reshape(ROWS, CW), w1[i // 4, q, :, cols])
            return 0

        lax.fori_loop(0, 2 * FF // TILE, tile, 0)

    for slot in range(2 * NC + far_k):
        for q in range(NC):
            k = slot - 2 * q
            if 0 <= k <= far_k:
                ag_step(q, k)
        done = slot - far_k
        if done >= 0 and done % 2 == 0 and done // 2 < NC:
            select(done // 2)
            if done // 2 >= 1:
                expert_up(done // 2 - 1)
    expert_up(NC - 1)

    for n in range(FF // TILE):
        gate = acc[n]
        act[:, n * TILE:(n + 1) * TILE] = (gate / (1.0 + jnp.exp(-gate)) * acc[FF // TILE + n]).astype(BF16)

    pltpu.make_async_copy(w2, w2, w_sem.at[1]).wait()
    order = [(i + (y + 1) * PER_Y) % NC for i in range(NC)]
    rt = {}
    for i in range(NC):
        q = order[i]

        def tile(n, _, q=q, i=i):
            cols = pl.ds(pl.multiple_of(n * TILE, TILE), TILE)
            value = nn(act[...], w2[q, :, cols]).astype(BF16)
            yout[i, :, :, cols] = value.reshape(XS * CS, GROUP, TILE)
            return 0

        lax.fori_loop(0, CW // TILE, tile, 0)
        for j, (dx, dc) in enumerate(PEERS):
            xx, cc = (x + dx) % XS, (c + dc) % CS
            rt[i, j] = go(remote(yout.at[i, xx * CS + cc], ret.at[i, mine_d], rt_send.at[i, j],
                                 rt_recv.at[i, j], seq=seq_id(xx, z, cc)))
        own = pltpu.make_async_copy(yout.at[i, mine_d], ret.at[i, mine_d], loc_sem.at[1, i])
        own.start()
        rt[i, "own"] = own

    rs = {}

    def rs_left(i, step):
        k = far_k + 1 - step
        value = part[i, k]
        if step > 1:
            rs["l", i, step - 1].wait_recv()
            value = value + rs_recv[i, step - 2].astype(F32)
        rs_send[i, step - 1] = value.astype(BF16)
        rs["l", i, step] = go(remote(rs_send.at[i, step - 1], rs_recv.at[i, step - 1],
                                     rs_ssem.at[i, step - 1], rs_rsem.at[i, step - 1], seq=left))

    def rs_right(i, step):
        k = far_k + step
        at = far_k + step - 1
        value = part[i, k]
        if step > 1:
            rs["r", i, step - 1].wait_recv()
            value = value + rs_recv[i, at - 1].astype(F32)
        rs_send[i, at] = value.astype(BF16)
        rs["r", i, step] = go(remote(rs_send.at[i, at], rs_recv.at[i, at],
                                     rs_ssem.at[i, at], rs_rsem.at[i, at], seq=right))

    def rs_step(i, step):
        if step == 1:
            for j in range(len(PEERS)):
                rt[i, j].wait_recv()
            rt[i, "own"].wait()
            answers = ret[i].reshape(ROWS, CW)
            part[i] = (nn(mixhi[...], answers) + nn(mixlo[...], answers)).reshape(ZS, SUB, CW)
        if step <= far_k:
            rs_left(i, step)
        if step < far_k:
            rs_right(i, step)
        if step == far_k + 1:
            rs["l", i, far_k].wait_recv()
            rs["r", i, far_k - 1].wait_recv()
            total = (part[i, 0] + rs_recv[i, far_k - 1].astype(F32) + rs_recv[i, ZS - 2].astype(F32)).astype(BF16)
            mine[i] = total
            if i < NC - PER_Y:
                peer = (y + 1 + i // PER_Y) % YS
                rs["y", i] = go(remote(mine.at[i], moe.at[y, i % PER_Y], fy_send.at[i], fy_recv.at[i], exp=peer))
            else:
                moe[y, i % PER_Y] = total

    for slot in range(3 * NC + far_k + 1):
        for i in range(NC):
            step = slot - 3 * i + 1
            if 1 <= step <= far_k + 1:
                rs_step(i, step)

    for i in range(NC - PER_Y):
        rs["y", i].wait_recv()
    for j in range(YS):
        for p in range(PER_Y):
            cols = pl.ds(p * CW, CW)
            sub = pl.ds(j * SUB, SUB)
            out_ref[sub, cols] = (hidden[sub, cols].astype(F32) + moe[j, p].astype(F32)).astype(BF16)

    remote(others(state), others(gathered), st_send, st_recv).wait_send()
    remote(others(running), others(prior), pr_send, pr_recv).wait_send()
    for copy in pending:
        copy.wait_send()


def per_device(residual, queries, key_vectors, value_vectors, head_gain, norm_gain, routes, route_gates,
               expert_in, expert_out):
    vmem = pl.BlockSpec(memory_space=pltpu.VMEM)
    hbm = pl.BlockSpec(memory_space=pl.ANY)
    dma = pltpu.SemaphoreType.DMA
    peers = len(PEERS)
    return pl.pallas_call(
        layer_kernel,
        out_shape=jax.ShapeDtypeStruct(residual.shape, BF16),
        in_specs=[vmem] * 8 + [hbm] * 2,
        out_specs=vmem,
        scratch_shapes=[
            pltpu.VMEM((2, NC, CW, FF), BF16),
            pltpu.VMEM((NC, FF, CW), BF16),
            pltpu.VMEM((SEQ, 8, HEAD), F32),
            pltpu.VMEM((SEQ, 8, HEAD), F32),
            pltpu.VMEM((SEQ, 8, HEAD), F32),
            pltpu.VMEM((SEQ, 8, HEAD), F32),
            pltpu.VMEM(residual.shape, F32),
            pltpu.VMEM(residual.shape, BF16),
            pltpu.VMEM((YS, SUB, D // YS), BF16),
            pltpu.VMEM((ZS, SUB, 128), F32),
            pltpu.VMEM((ROWS, ZS * SUB), BF16),
            pltpu.VMEM((ZS * SUB, ROWS), BF16),
            pltpu.VMEM((ZS * SUB, ROWS), BF16),
            pltpu.VMEM((NC, ZS, SUB, CW), BF16),
            pltpu.VMEM((NC, XS * CS, GROUP, CW), BF16),
            pltpu.VMEM((NC, XS * CS, GROUP, CW), BF16),
            pltpu.VMEM((2 * FF // TILE, ROWS, TILE), F32),
            pltpu.VMEM((ROWS, FF), BF16),
            pltpu.VMEM((NC, XS * CS, GROUP, CW), BF16),
            pltpu.VMEM((NC, XS * CS, GROUP, CW), BF16),
            pltpu.VMEM((NC, ZS, SUB, CW), F32),
            pltpu.VMEM((NC, ZS - 1, SUB, CW), BF16),
            pltpu.VMEM((NC, ZS - 1, SUB, CW), BF16),
            pltpu.VMEM((NC, SUB, CW), BF16),
            pltpu.VMEM((YS, PER_Y, SUB, CW), BF16),
            dma((2,)), dma, dma, dma, dma,
            dma((ZS - 1,)), dma((ZS - 1,)),
            dma((YS - 1,)), dma((YS - 1,)),
            dma((NC, ZS - 1)), dma((NC, ZS - 1)),
            dma((NC, peers)), dma((NC, peers)),
            dma((2, NC)),
            dma((NC, peers)), dma((NC, peers)),
            dma((NC, ZS - 1)), dma((NC, ZS - 1)),
            dma((NC,)), dma((NC,)),
        ],
        compiler_params=pltpu.CompilerParams(
            collective_id=0, has_side_effects=True, vmem_limit_bytes=60 * 1024 * 1024),
        name="layer",
    )(queries, key_vectors, value_vectors, residual, head_gain.reshape(1, -1), norm_gain.reshape(1, -1),
      routes, route_gates, expert_in, expert_out)


def solution(mesh):
    placed = (
        P("seq", "exp"), P("seq", "exp"), P("seq", "exp"), P("seq", "exp"), P("exp"), P(),
        P("seq", None), P("seq", None), P("seq", None, None, None), P("seq", None, None),
    )
    return jax.shard_map(
        per_device, mesh=mesh, in_specs=placed, out_specs=P("seq", "exp"), check_vma=False
    )
```

```python
import functools

import jax
import jax.numpy as jnp
from jax import lax
from jax.experimental import pallas as pl
from jax.experimental.pallas import tpu as pltpu
from jax.sharding import PartitionSpec as P

MESH = pl.DeviceIdType.MESH
F32 = jnp.float32
BF16 = jnp.bfloat16

HEAD = 128
XS, ZS, CS, YS = 4, 8, 2, 4
SEQ = XS * ZS * CS
D = 2048
FF = 1024
SUB = 32
CAP = 6
NC = 4
CW = D // NC
PER_Y = NC // YS
HALF = ZS // 2
GROUP = HALF * CAP
HROWS = XS * CS * GROUP
ROWS = 2 * HROWS
TILE = 256
PEERS = ((2, 0), (2, 1), (1, 0), (3, 0), (1, 1), (3, 1), (0, 1))


def nt(a, b):
    return lax.dot_general(a, b, (((1,), (1,)), ((), ())), preferred_element_type=F32)


def tn(a, b):
    return lax.dot_general(a, b, (((0,), (0,)), ((), ())), preferred_element_type=F32)


def nn(a, b):
    return jnp.dot(a, b, preferred_element_type=F32)


def halves(value):
    high = value.astype(BF16)
    return high, (value - high.astype(F32)).astype(BF16)


def layer_kernel(
    q_ref, k_ref, v_ref, res_ref, hgain_ref, ngain_ref, routes_ref, gates_ref, win_ref, wout_ref,
    out_ref,
    w1, w2, state, gathered, running, prior, raw, hidden, rows, meta, place, mixhi, mixlo,
    blk, sel, xin, acc, act, yout, ret, part, rs_send, rs_recv, mine, moe,
    w_sem, st_send, st_recv, pr_send, pr_recv, meta_send, meta_recv, y_send, y_recv,
    ag_send, ag_recv, xs_send, xs_recv, loc_sem, rt_send, rt_recv, rs_ssem, rs_rsem, fy_send, fy_recv,
):
    me = lax.axis_index("seq")
    y = lax.axis_index("exp")
    x = me // (ZS * CS)
    z = (me // CS) % ZS
    c = me % CS
    mine_d = x * CS + c

    def seq_id(xx, zz, cc):
        return (xx * ZS + zz) * CS + cc

    def remote(src, dst, ssem, rsem, seq=None, exp=None):
        return pltpu.make_async_remote_copy(
            src_ref=src, dst_ref=dst, send_sem=ssem, recv_sem=rsem,
            device_id=(me if seq is None else seq, y if exp is None else exp),
            device_id_type=MESH,
        )

    pending = []

    def go(copy):
        copy.start()
        pending.append(copy)
        return copy

    weights = []
    for q in range(NC):
        for g in range(2):
            weights.append(pltpu.make_async_copy(
                win_ref.at[0, g, pl.ds(q * CW, CW), :], w1.at[g, q], w_sem.at[0]))
    for q in range(NC):
        weights.append(pltpu.make_async_copy(
            wout_ref.at[0, :, pl.ds(q * CW, CW)], w2.at[q], w_sem.at[1]))
    for copy in weights:
        copy.start()

    barrier = pltpu.get_barrier_semaphore()

    def greet(i, _):
        pl.semaphore_signal(barrier, inc=1, device_id=((me + i) % SEQ, y), device_id_type=MESH)
        return 0

    lax.fori_loop(1, SEQ, greet, 0)
    for j in range(1, YS):
        pl.semaphore_signal(barrier, inc=1, device_id=(me, (y + j) % YS), device_id_type=MESH)

    heads = q_ref.shape[1] // HEAD
    for h in range(heads):
        cols = pl.ds(h * HEAD, HEAD)
        outer = tn(k_ref[:, cols], v_ref[:, cols])
        state[pl.ds(h * 16, 16)] = outer.reshape(16, 8, HEAD).astype(BF16)

    pl.semaphore_wait(barrier, SEQ - 1 + YS - 1)

    def send_state(i, _):
        for peer in ((me + i) % SEQ, (me + SEQ - i) % SEQ):
            remote(state.at[peer], gathered.at[me], st_send, st_recv, seq=peer).start()
        return 0

    lax.fori_loop(1, SEQ // 2, send_state, 0)
    far = (me + SEQ // 2) % SEQ
    remote(state.at[far], gathered.at[me], st_send, st_recv, seq=far).start()
    gathered[me] = state[me]

    tok = lax.broadcasted_iota(jnp.int32, (128, 128), 1)
    row = lax.broadcasted_iota(jnp.int32, (128, 128), 0)
    onehot = jnp.zeros((128, 128), F32)
    gate_rows = jnp.zeros((128, 128), F32)
    for k in range(routes_ref.shape[0]):
        route = routes_ref[k:k + 1, :]
        onehot = onehot + jnp.where(route == row, 1.0, 0.0)
        gate_rows = gate_rows + jnp.where(route + 64 == row, gates_ref[k:k + 1, :], 0.0)
    earlier = jnp.where((row < tok) & ((row >> 5) == (tok >> 5)), 1.0, 0.0).astype(BF16)
    table = onehot * (nn(onehot.astype(BF16), earlier) + 1.0) + gate_rows
    take = jnp.where(
        lax.broadcasted_iota(jnp.int32, (SUB, 128), 1) == lax.broadcasted_iota(jnp.int32, (SUB, 128), 0) + y * SUB,
        1.0, 0.0).astype(BF16)
    high, low = halves(table)
    meta[1] = nt(take, high) + nt(take, low)
    for k in range(1, ZS):
        go(remote(meta.at[1], meta.at[(k + 1) % ZS], meta_send.at[k - 1], meta_recv.at[k - 1],
                  seq=seq_id(x, (z + k) % ZS, c)))

    causal = row >= tok
    for h in range(heads):
        cols = pl.ds(h * HEAD, HEAD)
        scores = jnp.where(causal, nt(q_ref[:, cols], k_ref[:, cols]), 0.0)
        high, low = halves(scores)
        raw[:, cols] = nn(high, v_ref[:, cols]) + nn(low, v_ref[:, cols])

    def others(ref):
        return ref.at[pl.ds(0, SEQ - 1)]

    remote(others(state), others(gathered), st_send, st_recv).wait_recv()

    def scan_step(s, total):
        running[s] = total.astype(BF16)
        return total + gathered[s].astype(F32)

    lax.fori_loop(0, SEQ, scan_step, jnp.zeros((8, HEAD), F32))

    def send_prior(i, _):
        for peer in ((me + i) % SEQ, (me + SEQ - i) % SEQ):
            remote(running.at[peer], prior.at[me], pr_send, pr_recv, seq=peer).start()
        return 0

    lax.fori_loop(1, SEQ // 2, send_prior, 0)
    remote(running.at[far], prior.at[me], pr_send, pr_recv, seq=far).start()
    prior[me] = running[me]

    for copy in pending[:ZS - 1]:
        copy.wait_recv()
    everyone = meta[...].reshape(ZS * SUB, 128)
    meta_hi, meta_lo = halves(everyone)

    def slot_parts(shape, dim):
        index = lax.broadcasted_iota(jnp.int32, shape, dim)
        group = (index * 10923) >> 16
        return group >> 2, group & 3, index - group * CAP

    d_of, _, _ = slot_parts((HROWS, 128), 0)
    expert_of = seq_id(d_of >> 1, z, d_of & 1)
    lanes = lax.broadcasted_iota(jnp.int32, (HROWS, 128), 1)
    pick_rank = jnp.where(lanes == expert_of, 1.0, 0.0).astype(BF16)
    pick_gate = jnp.where(lanes == expert_of + 64, 1.0, 0.0).astype(BF16)
    _, k_row, r_row = slot_parts((HROWS, 128), 0)
    k_col = lanes >> 5
    _, mk_row, mr_row = slot_parts((128, HROWS), 1)
    mk_col = lax.broadcasted_iota(jnp.int32, (128, HROWS), 0) >> 5
    for hf in range(2):
        hi_part, lo_part = meta_hi[hf * 128:(hf + 1) * 128], meta_lo[hf * 128:(hf + 1) * 128]
        found = (nt(pick_rank, hi_part) == (r_row + 1).astype(F32)) & (k_row == k_col)
        place[hf] = jnp.where(found, 1.0, 0.0).astype(BF16)
        found = (nt(hi_part, pick_rank) == (mr_row + 1).astype(F32)) & (mk_row == mk_col)
        mix = jnp.where(found, nt(hi_part, pick_gate) + nt(lo_part, pick_gate), 0.0)
        high, low = halves(mix)
        mixhi[hf] = high
        mixlo[hf] = low
    acc[...] = jnp.zeros(acc.shape, F32)

    remote(others(running), others(prior), pr_send, pr_recv).wait_recv()
    for h in range(heads):
        cols = pl.ds(h * HEAD, HEAD)
        before = prior[pl.ds(h * 16, 16)].astype(F32).reshape(HEAD, HEAD).astype(BF16)
        total = nn(q_ref[:, cols], before) + raw[:, cols]
        scale = lax.rsqrt(jnp.mean(total * total, axis=1, keepdims=True) + 1e-6)
        hidden[:, cols] = (res_ref[:, cols].astype(F32) + total * scale * hgain_ref[:, cols]).astype(BF16)

    y_copies = []
    for j in range(1, YS):
        peer = (y + j) % YS
        y_copies.append(go(remote(
            hidden.at[pl.ds(pl.multiple_of(peer * SUB, SUB), SUB), :], rows.at[y],
            y_send.at[j - 1], y_recv.at[j - 1], exp=peer)))
    rows[y] = hidden[pl.ds(pl.multiple_of(y * SUB, SUB), SUB), :]
    for copy in y_copies:
        copy.wait_recv()
    wide = [rows[j].astype(F32) for j in range(YS)]
    square = sum(jnp.sum(w * w, axis=1, keepdims=True) for w in wide)
    scale = lax.rsqrt(square * (1.0 / D) + 1e-6)
    for q in range(NC):
        part_cols = wide[q // PER_Y][:, (q % PER_Y) * CW:(q % PER_Y + 1) * CW]
        blk[q, 1] = (part_cols * scale * ngain_ref[:, q * CW:(q + 1) * CW]).astype(BF16)

    right = seq_id(x, (z + 1) % ZS, c)
    left = seq_id(x, (z + ZS - 1) % ZS, c)
    far_k = ZS // 2
    ag = {}

    def at(k):
        return (k + 1) % ZS

    def ag_right(q, k):
        ag["r", q, k] = go(remote(blk.at[q, at(k - 1)], blk.at[q, at(k)], ag_send.at[q, k - 1],
                                  ag_recv.at[q, k - 1], seq=right))

    def ag_left(q, k):
        ag["l", q, k] = go(remote(blk.at[q, at(ZS - k + 1)], blk.at[q, at(ZS - k)], ag_send.at[q, ZS - k - 1],
                                  ag_recv.at[q, ZS - k - 1], seq=left))

    def ag_step(q, k):
        if k > 0:
            ag["r", q, k].wait_recv()
        if k < far_k:
            ag_right(q, k + 1)
        if 0 < k < far_k:
            ag["l", q, k].wait_recv()
        if k + 1 < far_k:
            ag_left(q, k + 1)

    xs = {}

    def select(q, hf):
        source = blk[q, hf * HALF:(hf + 1) * HALF].reshape(HALF * SUB, CW)
        sel[q, hf] = nn(place[hf], source).astype(BF16).reshape(XS * CS, GROUP, CW)
        for j, (dx, dc) in enumerate(PEERS):
            xx, cc = (x + dx) % XS, (c + dc) % CS
            xs[q, hf, j] = go(remote(sel.at[q, hf, xx * CS + cc], xin.at[q, hf, mine_d], xs_send.at[q, hf, j],
                                     xs_recv.at[q, hf, j], seq=seq_id(xx, z, cc)))
        own = pltpu.make_async_copy(sel.at[q, hf, mine_d], xin.at[q, hf, mine_d], loc_sem.at[0, q, hf])
        own.start()
        xs[q, hf, "own"] = own

    def expert_up(q):
        if q == 0:
            pltpu.make_async_copy(w1, w1, w_sem.at[0]).wait()
        for hf in range(2):
            for j in range(len(PEERS)):
                xs[q, hf, j].wait_recv()
            xs[q, hf, "own"].wait()

        def tile(i, _):
            cols = pl.ds(pl.multiple_of((i % 4) * TILE, TILE), TILE)
            acc[i] += nn(xin[q].reshape(ROWS, CW), w1[i // 4, q, :, cols])
            return 0

        lax.fori_loop(0, 2 * FF // TILE, tile, 0)

    for q in range(NC):
        ag_step(q, 0)
    for k in range(1, far_k + 1):
        for q in range(NC):
            ag_step(q, k)
            if k == 2:
                select(q, 0)
            if k == far_k:
                select(q, 1)
    for q in range(NC):
        expert_up(q)

    for n in range(FF // TILE):
        gate = acc[n]
        act[:, n * TILE:(n + 1) * TILE] = (gate / (1.0 + jnp.exp(-gate)) * acc[FF // TILE + n]).astype(BF16)

    pltpu.make_async_copy(w2, w2, w_sem.at[1]).wait()
    order = [(i + (y + 1) * PER_Y) % NC for i in range(NC)]
    rt = {}

    def send_back(i, hf):
        for j, (dx, dc) in enumerate(PEERS):
            xx, cc = (x + dx) % XS, (c + dc) % CS
            rt[i, hf, j] = go(remote(yout.at[i, hf, xx * CS + cc], ret.at[i, hf, mine_d], rt_send.at[i, hf, j],
                                     rt_recv.at[i, hf, j], seq=seq_id(xx, z, cc)))
        own = pltpu.make_async_copy(yout.at[i, hf, mine_d], ret.at[i, hf, mine_d], loc_sem.at[1, i, hf])
        own.start()
        rt[i, hf, "own"] = own

    for i in range(NC):
        q = order[i]

        def tile(n, _, q=q, i=i):
            cols = pl.ds(pl.multiple_of(n * TILE, TILE), TILE)
            value = nn(act[...], w2[q, :, cols]).astype(BF16)
            yout[i, :, :, :, cols] = value.reshape(2, XS * CS, GROUP, TILE)
            return 0

        lax.fori_loop(0, CW // TILE, tile, 0)
        send_back(i, 1)
    for i in range(NC):
        send_back(i, 0)

    rs = {}

    def answers(i, hf):
        for j in range(len(PEERS)):
            rt[i, hf, j].wait_recv()
        rt[i, hf, "own"].wait()
        value = ret[i, hf].reshape(HROWS, CW)
        part[i, hf] = (nn(mixhi[hf], value) + nn(mixlo[hf], value)).reshape(HALF, SUB, CW)

    def own_part(i, k):
        return part[i, at(k) // HALF, at(k) % HALF]

    def rs_left(i, step):
        value = own_part(i, far_k + 1 - step)
        if step > 1:
            rs["l", i, step - 1].wait_recv()
            value = value + rs_recv[i, step - 2].astype(F32)
        rs_send[i, step - 1] = value.astype(BF16)
        rs["l", i, step] = go(remote(rs_send.at[i, step - 1], rs_recv.at[i, step - 1],
                                     rs_ssem.at[i, step - 1], rs_rsem.at[i, step - 1], seq=left))

    def rs_right(i, step):
        slot = far_k + step - 1
        value = own_part(i, far_k + step)
        if step > 1:
            rs["r", i, step - 1].wait_recv()
            value = value + rs_recv[i, slot - 1].astype(F32)
        rs_send[i, slot] = value.astype(BF16)
        rs["r", i, step] = go(remote(rs_send.at[i, slot], rs_recv.at[i, slot],
                                     rs_ssem.at[i, slot], rs_rsem.at[i, slot], seq=right))

    def rs_step(i, step):
        if step == 1:
            answers(i, 1)
        if step == 3:
            answers(i, 0)
        if step <= far_k:
            rs_left(i, step)
        if step < far_k:
            rs_right(i, step)
        if step == far_k + 1:
            rs["l", i, far_k].wait_recv()
            rs["r", i, far_k - 1].wait_recv()
            total = (own_part(i, 0) + rs_recv[i, far_k - 1].astype(F32) + rs_recv[i, ZS - 2].astype(F32)).astype(BF16)
            mine[i] = total
            if i < NC - PER_Y:
                peer = (y + 1 + i // PER_Y) % YS
                rs["y", i] = go(remote(mine.at[i], moe.at[y, i % PER_Y], fy_send.at[i], fy_recv.at[i], exp=peer))
            else:
                moe[y, i % PER_Y] = total

    spacing = 8.8 / NC
    events = []
    for i in range(NC):
        first, second = spacing * (i + 1), spacing * (NC + i + 1)
        for step, when in ((1, first), (2, first + 2.8), (3, second), (4, second + 2.8), (5, second + 5.6)):
            events.append((when, i, step))
    for when, i, step in sorted(events):
        rs_step(i, step)

    for i in range(NC - PER_Y):
        rs["y", i].wait_recv()
    for j in range(YS):
        for p in range(PER_Y):
            cols = pl.ds(p * CW, CW)
            sub = pl.ds(j * SUB, SUB)
            out_ref[sub, cols] = (hidden[sub, cols].astype(F32) + moe[j, p].astype(F32)).astype(BF16)

    remote(others(state), others(gathered), st_send, st_recv).wait_send()
    remote(others(running), others(prior), pr_send, pr_recv).wait_send()
    for copy in pending:
        copy.wait_send()


def per_device(residual, queries, key_vectors, value_vectors, head_gain, norm_gain, routes, route_gates,
               expert_in, expert_out):
    vmem = pl.BlockSpec(memory_space=pltpu.VMEM)
    hbm = pl.BlockSpec(memory_space=pl.ANY)
    dma = pltpu.SemaphoreType.DMA
    peers = len(PEERS)
    return pl.pallas_call(
        layer_kernel,
        out_shape=jax.ShapeDtypeStruct(residual.shape, BF16),
        in_specs=[vmem] * 8 + [hbm] * 2,
        out_specs=vmem,
        scratch_shapes=[
            pltpu.VMEM((2, NC, CW, FF), BF16),
            pltpu.VMEM((NC, FF, CW), BF16),
            pltpu.VMEM((SEQ, 8, HEAD), BF16),
            pltpu.VMEM((SEQ, 8, HEAD), BF16),
            pltpu.VMEM((SEQ, 8, HEAD), BF16),
            pltpu.VMEM((SEQ, 8, HEAD), BF16),
            pltpu.VMEM(residual.shape, F32),
            pltpu.VMEM(residual.shape, BF16),
            pltpu.VMEM((YS, SUB, D // YS), BF16),
            pltpu.VMEM((ZS, SUB, 128), F32),
            pltpu.VMEM((2, HROWS, HALF * SUB), BF16),
            pltpu.VMEM((2, HALF * SUB, HROWS), BF16),
            pltpu.VMEM((2, HALF * SUB, HROWS), BF16),
            pltpu.VMEM((NC, ZS, SUB, CW), BF16),
            pltpu.VMEM((NC, 2, XS * CS, GROUP, CW), BF16),
            pltpu.VMEM((NC, 2, XS * CS, GROUP, CW), BF16),
            pltpu.VMEM((2 * FF // TILE, ROWS, TILE), F32),
            pltpu.VMEM((ROWS, FF), BF16),
            pltpu.VMEM((NC, 2, XS * CS, GROUP, CW), BF16),
            pltpu.VMEM((NC, 2, XS * CS, GROUP, CW), BF16),
            pltpu.VMEM((NC, 2, HALF, SUB, CW), F32),
            pltpu.VMEM((NC, ZS - 1, SUB, CW), BF16),
            pltpu.VMEM((NC, ZS - 1, SUB, CW), BF16),
            pltpu.VMEM((NC, SUB, CW), BF16),
            pltpu.VMEM((YS, PER_Y, SUB, CW), BF16),
            dma((2,)), dma, dma, dma, dma,
            dma((ZS - 1,)), dma((ZS - 1,)),
            dma((YS - 1,)), dma((YS - 1,)),
            dma((NC, ZS - 1)), dma((NC, ZS - 1)),
            dma((NC, 2, peers)), dma((NC, 2, peers)),
            dma((2, NC, 2)),
            dma((NC, 2, peers)), dma((NC, 2, peers)),
            dma((NC, ZS - 1)), dma((NC, ZS - 1)),
            dma((NC,)), dma((NC,)),
        ],
        compiler_params=pltpu.CompilerParams(
            collective_id=0, has_side_effects=True, vmem_limit_bytes=60 * 1024 * 1024),
        name="layer",
    )(queries, key_vectors, value_vectors, residual, head_gain.reshape(1, -1), norm_gain.reshape(1, -1),
      routes.T, route_gates.T, expert_in, expert_out)


def solution(mesh):
    placed = (
        P("seq", "exp"), P("seq", "exp"), P("seq", "exp"), P("seq", "exp"), P("exp"), P(),
        P("seq", None), P("seq", None), P("seq", None, None, None), P("seq", None, None),
    )
    return jax.shard_map(
        per_device, mesh=mesh, in_specs=placed, out_specs=P("seq", "exp"), check_vma=False
    )
```

```python
import functools

import jax
import jax.numpy as jnp
from jax import lax
from jax.experimental import pallas as pl
from jax.experimental.pallas import tpu as pltpu
from jax.sharding import PartitionSpec as P

MESH = pl.DeviceIdType.MESH
F32 = jnp.float32
BF16 = jnp.bfloat16

HEAD = 128
XS, ZS, CS, YS = 4, 8, 2, 4
SEQ = XS * ZS * CS
D = 2048
FF = 1024
SUB = 32
CAP = 6
NC = 4
CW = D // NC
PER_Y = NC // YS
HALF = ZS // 2
GROUP = HALF * CAP
HROWS = XS * CS * GROUP
ROWS = 2 * HROWS
TILE = 256
PEERS = ((2, 0), (2, 1), (1, 0), (3, 0), (1, 1), (3, 1), (0, 1))


def nt(a, b):
    return lax.dot_general(a, b, (((1,), (1,)), ((), ())), preferred_element_type=F32)


def tn(a, b):
    return lax.dot_general(a, b, (((0,), (0,)), ((), ())), preferred_element_type=F32)


def nn(a, b):
    return jnp.dot(a, b, preferred_element_type=F32)


def halves(value):
    high = value.astype(BF16)
    return high, (value - high.astype(F32)).astype(BF16)


def layer_kernel(
    q_ref, k_ref, v_ref, res_ref, hgain_ref, ngain_ref, routes_ref, gates_ref, win_ref, wout_ref,
    out_ref,
    w1, w2, state, gathered, running, prior, raw, hidden, rows, meta, place, mixhi, mixlo,
    blk, sel, xin, acc, act, yout, ret, part, rs_send, rs_recv, mine, moe,
    w_sem, st_send, st_recv, pr_send, pr_recv, meta_send, meta_recv, y_send, y_recv,
    ag_send, ag_recv, xs_send, xs_recv, loc_sem, rt_send, rt_recv, rs_ssem, rs_rsem, fy_send, fy_recv,
):
    me = lax.axis_index("seq")
    y = lax.axis_index("exp")
    x = me // (ZS * CS)
    z = (me // CS) % ZS
    c = me % CS
    mine_d = x * CS + c

    def seq_id(xx, zz, cc):
        return (xx * ZS + zz) * CS + cc

    def remote(src, dst, ssem, rsem, seq=None, exp=None):
        return pltpu.make_async_remote_copy(
            src_ref=src, dst_ref=dst, send_sem=ssem, recv_sem=rsem,
            device_id=(me if seq is None else seq, y if exp is None else exp),
            device_id_type=MESH,
        )

    pending = []

    def go(copy):
        copy.start()
        pending.append(copy)
        return copy

    weights = []
    for q in range(NC):
        for g in range(2):
            weights.append(pltpu.make_async_copy(
                win_ref.at[0, g, pl.ds(q * CW, CW), :], w1.at[g, q], w_sem.at[0]))
    for q in range(NC):
        weights.append(pltpu.make_async_copy(
            wout_ref.at[0, :, pl.ds(q * CW, CW)], w2.at[q], w_sem.at[1]))
    for copy in weights:
        copy.start()

    barrier = pltpu.get_barrier_semaphore()

    def greet(i, _):
        pl.semaphore_signal(barrier, inc=1, device_id=((me + i) % SEQ, y), device_id_type=MESH)
        return 0

    lax.fori_loop(1, SEQ, greet, 0)
    for j in range(1, YS):
        pl.semaphore_signal(barrier, inc=1, device_id=(me, (y + j) % YS), device_id_type=MESH)

    heads = q_ref.shape[1] // HEAD
    for h in range(heads):
        cols = pl.ds(h * HEAD, HEAD)
        outer = tn(k_ref[:, cols], v_ref[:, cols])
        state[pl.ds(h * 16, 16)] = outer.reshape(16, 8, HEAD).astype(BF16)

    pl.semaphore_wait(barrier, SEQ - 1 + YS - 1)

    def send_state(i, _):
        for peer in ((me + i) % SEQ, (me + SEQ - i) % SEQ):
            remote(state.at[peer], gathered.at[me], st_send, st_recv, seq=peer).start()
        return 0

    lax.fori_loop(1, SEQ // 2, send_state, 0)
    far = (me + SEQ // 2) % SEQ
    remote(state.at[far], gathered.at[me], st_send, st_recv, seq=far).start()
    gathered[me] = state[me]

    tok = lax.broadcasted_iota(jnp.int32, (128, 128), 1)
    row = lax.broadcasted_iota(jnp.int32, (128, 128), 0)
    onehot = jnp.zeros((128, 128), F32)
    gate_rows = jnp.zeros((128, 128), F32)
    for k in range(routes_ref.shape[0]):
        route = routes_ref[k:k + 1, :]
        onehot = onehot + jnp.where(route == row, 1.0, 0.0)
        gate_rows = gate_rows + jnp.where(route + 64 == row, gates_ref[k:k + 1, :], 0.0)
    earlier = jnp.where((row < tok) & ((row >> 5) == (tok >> 5)), 1.0, 0.0).astype(BF16)
    table = onehot * (nn(onehot.astype(BF16), earlier) + 1.0) + gate_rows
    take = jnp.where(
        lax.broadcasted_iota(jnp.int32, (SUB, 128), 1) == lax.broadcasted_iota(jnp.int32, (SUB, 128), 0) + y * SUB,
        1.0, 0.0).astype(BF16)
    high, low = halves(table)
    meta[1] = nt(take, high) + nt(take, low)
    for k in range(1, ZS):
        go(remote(meta.at[1], meta.at[(k + 1) % ZS], meta_send.at[k - 1], meta_recv.at[k - 1],
                  seq=seq_id(x, (z + k) % ZS, c)))

    causal = row >= tok
    for h in range(heads):
        cols = pl.ds(h * HEAD, HEAD)
        scores = jnp.where(causal, nt(q_ref[:, cols], k_ref[:, cols]), 0.0)
        high, low = halves(scores)
        raw[:, cols] = nn(high, v_ref[:, cols]) + nn(low, v_ref[:, cols])

    def others(ref):
        return ref.at[pl.ds(0, SEQ - 1)]

    remote(others(state), others(gathered), st_send, st_recv).wait_recv()

    def scan_step(s, total):
        running[s] = total.astype(BF16)
        return total + gathered[s].astype(F32)

    lax.fori_loop(0, SEQ, scan_step, jnp.zeros((8, HEAD), F32))

    def send_prior(i, _):
        for peer in ((me + i) % SEQ, (me + SEQ - i) % SEQ):
            remote(running.at[peer], prior.at[me], pr_send, pr_recv, seq=peer).start()
        return 0

    lax.fori_loop(1, SEQ // 2, send_prior, 0)
    remote(running.at[far], prior.at[me], pr_send, pr_recv, seq=far).start()
    prior[me] = running[me]

    for copy in pending[:ZS - 1]:
        copy.wait_recv()
    everyone = meta[...].reshape(ZS * SUB, 128)
    meta_hi, meta_lo = halves(everyone)

    def slot_parts(shape, dim):
        index = lax.broadcasted_iota(jnp.int32, shape, dim)
        group = (index * 10923) >> 16
        return group >> 2, group & 3, index - group * CAP

    d_of, _, _ = slot_parts((HROWS, 128), 0)
    expert_of = seq_id(d_of >> 1, z, d_of & 1)
    lanes = lax.broadcasted_iota(jnp.int32, (HROWS, 128), 1)
    pick_rank = jnp.where(lanes == expert_of, 1.0, 0.0).astype(BF16)
    pick_gate = jnp.where(lanes == expert_of + 64, 1.0, 0.0).astype(BF16)
    _, k_row, r_row = slot_parts((HROWS, 128), 0)
    k_col = lanes >> 5
    _, mk_row, mr_row = slot_parts((128, HROWS), 1)
    mk_col = lax.broadcasted_iota(jnp.int32, (128, HROWS), 0) >> 5
    for hf in range(2):
        hi_part, lo_part = meta_hi[hf * 128:(hf + 1) * 128], meta_lo[hf * 128:(hf + 1) * 128]
        found = (nt(pick_rank, hi_part) == (r_row + 1).astype(F32)) & (k_row == k_col)
        place[hf] = jnp.where(found, 1.0, 0.0).astype(BF16)
        found = (nt(hi_part, pick_rank) == (mr_row + 1).astype(F32)) & (mk_row == mk_col)
        mix = jnp.where(found, nt(hi_part, pick_gate) + nt(lo_part, pick_gate), 0.0)
        high, low = halves(mix)
        mixhi[hf] = high
        mixlo[hf] = low

    remote(others(running), others(prior), pr_send, pr_recv).wait_recv()
    for h in range(heads):
        cols = pl.ds(h * HEAD, HEAD)
        before = prior[pl.ds(h * 16, 16)].astype(F32).reshape(HEAD, HEAD).astype(BF16)
        total = nn(q_ref[:, cols], before) + raw[:, cols]
        scale = lax.rsqrt(jnp.mean(total * total, axis=1, keepdims=True) + 1e-6)
        hidden[:, cols] = (res_ref[:, cols].astype(F32) + total * scale * hgain_ref[:, cols]).astype(BF16)

    y_copies = []
    for j in range(1, YS):
        peer = (y + j) % YS
        y_copies.append(go(remote(
            hidden.at[pl.ds(pl.multiple_of(peer * SUB, SUB), SUB), :], rows.at[y],
            y_send.at[j - 1], y_recv.at[j - 1], exp=peer)))
    rows[y] = hidden[pl.ds(pl.multiple_of(y * SUB, SUB), SUB), :]
    for copy in y_copies:
        copy.wait_recv()
    wide = [rows[j].astype(F32) for j in range(YS)]
    square = sum(jnp.sum(w * w, axis=1, keepdims=True) for w in wide)
    scale = lax.rsqrt(square * (1.0 / D) + 1e-6)
    for q in range(NC):
        part_cols = wide[q // PER_Y][:, (q % PER_Y) * CW:(q % PER_Y + 1) * CW]
        blk[q, 1] = (part_cols * scale * ngain_ref[:, q * CW:(q + 1) * CW]).astype(BF16)

    right = seq_id(x, (z + 1) % ZS, c)
    left = seq_id(x, (z + ZS - 1) % ZS, c)
    far_k = ZS // 2
    ag = {}

    def at(k):
        return (k + 1) % ZS

    def ag_right(q, k):
        ag["r", q, k] = go(remote(blk.at[q, at(k - 1)], blk.at[q, at(k)], ag_send.at[q, k - 1],
                                  ag_recv.at[q, k - 1], seq=right))

    def ag_left(q, k):
        ag["l", q, k] = go(remote(blk.at[q, at(ZS - k + 1)], blk.at[q, at(ZS - k)], ag_send.at[q, ZS - k - 1],
                                  ag_recv.at[q, ZS - k - 1], seq=left))

    def ag_step(q, k):
        if k > 0:
            ag["r", q, k].wait_recv()
        if k < far_k:
            ag_right(q, k + 1)
        if 0 < k < far_k:
            ag["l", q, k].wait_recv()
        if k + 1 < far_k:
            ag_left(q, k + 1)

    xs = {}

    def select(q, hf):
        source = blk[q, hf * HALF:(hf + 1) * HALF].reshape(HALF * SUB, CW)
        sel[q, hf] = nn(place[hf], source).astype(BF16).reshape(XS * CS, GROUP, CW)
        for j, (dx, dc) in enumerate(PEERS):
            xx, cc = (x + dx) % XS, (c + dc) % CS
            xs[q, hf, j] = go(remote(sel.at[q, hf, xx * CS + cc], xin.at[q, hf, mine_d], xs_send.at[q, hf, j],
                                     xs_recv.at[q, hf, j], seq=seq_id(xx, z, cc)))
        own = pltpu.make_async_copy(sel.at[q, hf, mine_d], xin.at[q, hf, mine_d], loc_sem.at[0, q, hf])
        own.start()
        xs[q, hf, "own"] = own

    def expert_up(q, hf):
        if q == 0 and hf == 0:
            pltpu.make_async_copy(w1, w1, w_sem.at[0]).wait()
        for j in range(len(PEERS)):
            xs[q, hf, j].wait_recv()
        xs[q, hf, "own"].wait()

        def tile(i, _):
            cols = pl.ds(pl.multiple_of((i % 4) * TILE, TILE), TILE)
            value = nn(xin[q, hf].reshape(HROWS, CW), w1[i // 4, q, :, cols])
            if q == 0:
                acc[hf, i] = value
            else:
                acc[hf, i] += value
            return 0

        lax.fori_loop(0, 2 * FF // TILE, tile, 0, unroll=2)

    def activate(hf):
        for n in range(FF // TILE):
            gate = acc[hf, n]
            act[hf, :, n * TILE:(n + 1) * TILE] = (
                gate / (1.0 + jnp.exp(-gate)) * acc[hf, FF // TILE + n]).astype(BF16)

    rt = {}
    order = [(i + (y + 1) * PER_Y) % NC for i in range(NC)]

    def expert_down(i, hf):
        for n in range(CW // TILE):
            cols = pl.ds(n * TILE, TILE)
            value = nn(act[hf], w2[order[i], :, cols]).astype(BF16)
            yout[i, hf, :, :, cols] = value.reshape(XS * CS, GROUP, TILE)
        for j, (dx, dc) in enumerate(PEERS):
            xx, cc = (x + dx) % XS, (c + dc) % CS
            rt[i, hf, j] = go(remote(yout.at[i, hf, xx * CS + cc], ret.at[i, hf, mine_d], rt_send.at[i, hf, j],
                                     rt_recv.at[i, hf, j], seq=seq_id(xx, z, cc)))
        own = pltpu.make_async_copy(yout.at[i, hf, mine_d], ret.at[i, hf, mine_d], loc_sem.at[1, i, hf])
        own.start()
        rt[i, hf, "own"] = own

    for q in range(NC):
        ag_step(q, 0)
    for k in range(1, far_k + 1):
        for q in range(NC):
            ag_step(q, k)
            if k == 2:
                select(q, 0)
            if k == far_k:
                select(q, 1)
    for q in range(NC):
        expert_up(q, 0)
    activate(0)
    pltpu.make_async_copy(w2, w2, w_sem.at[1]).wait()
    for i in range(NC // 2):
        expert_down(i, 0)
    for q in range(NC):
        expert_up(q, 1)
    activate(1)
    for i in range(NC):
        expert_down(i, 1)
    for i in range(NC // 2, NC):
        expert_down(i, 0)

    rs = {}

    def answers(i, hf):
        for j in range(len(PEERS)):
            rt[i, hf, j].wait_recv()
        rt[i, hf, "own"].wait()
        value = ret[i, hf].reshape(HROWS, CW)
        part[i, hf] = (nn(mixhi[hf], value) + nn(mixlo[hf], value)).reshape(HALF, SUB, CW)

    def own_part(i, k):
        return part[i, at(k) // HALF, at(k) % HALF]

    def send_sum(i, slot, value, shift):
        rs_send[i, slot] = value.astype(BF16)
        rs[i, slot] = go(remote(rs_send.at[i, slot], rs_recv.at[i, slot], rs_ssem.at[i, slot], rs_rsem.at[i, slot],
                                seq=seq_id(x, (z + shift) % ZS, c)))

    def far_rows(i):
        answers(i, 1)
        send_sum(i, 0, own_part(i, 4), ZS - 1)
        send_sum(i, 1, own_part(i, 5), 1)

    def far_sums(i):
        rs[i, 0].wait_recv()
        send_sum(i, 2, own_part(i, 3) + rs_recv[i, 0].astype(F32), ZS - 3)
        rs[i, 1].wait_recv()
        send_sum(i, 3, own_part(i, 6) + rs_recv[i, 1].astype(F32), 2)

    def near_rows(i):
        answers(i, 0)
        send_sum(i, 4, own_part(i, 2), ZS - 2)
        send_sum(i, 5, own_part(i, 1), ZS - 1)
        send_sum(i, 6, own_part(i, 7), 1)

    def finish(i):
        total = own_part(i, 0)
        for slot in range(2, ZS - 1):
            rs[i, slot].wait_recv()
            total = total + rs_recv[i, slot].astype(F32)
        total = total.astype(BF16)
        if i < NC - PER_Y:
            mine[i] = total
            peer = (y + 1 + i // PER_Y) % YS
            rs["y", i] = go(remote(mine.at[i], moe.at[y, i % PER_Y], fy_send.at[i], fy_recv.at[i], exp=peer))
        else:
            moe[y, i % PER_Y] = total

    half_time = 8.8
    spacing = half_time / NC
    events = []
    for i in range(NC):
        far_at = half_time / 2 + spacing * (i + 1)
        near_at = spacing * (i + 1) if i < NC // 2 else half_time + spacing * (i + 1)
        events.append((near_at, i, near_rows))
        events.append((far_at, i, far_rows))
        events.append((far_at + 2.8, i, far_sums))
        events.append((max(far_at + 6.7, near_at + 3.2), i, finish))
    for when, i, act_on in sorted(events, key=lambda event: event[:2]):
        act_on(i)

    for i in range(NC - PER_Y):
        rs["y", i].wait_recv()
    for j in range(YS):
        for p in range(PER_Y):
            cols = pl.ds(p * CW, CW)
            sub = pl.ds(j * SUB, SUB)
            out_ref[sub, cols] = (hidden[sub, cols].astype(F32) + moe[j, p].astype(F32)).astype(BF16)

    remote(others(state), others(gathered), st_send, st_recv).wait_send()
    remote(others(running), others(prior), pr_send, pr_recv).wait_send()
    for copy in pending:
        copy.wait_send()


def per_device(residual, queries, key_vectors, value_vectors, head_gain, norm_gain, routes, route_gates,
               expert_in, expert_out):
    vmem = pl.BlockSpec(memory_space=pltpu.VMEM)
    hbm = pl.BlockSpec(memory_space=pl.ANY)
    dma = pltpu.SemaphoreType.DMA
    peers = len(PEERS)
    return pl.pallas_call(
        layer_kernel,
        out_shape=jax.ShapeDtypeStruct(residual.shape, BF16),
        in_specs=[vmem] * 8 + [hbm] * 2,
        out_specs=vmem,
        scratch_shapes=[
            pltpu.VMEM((2, NC, CW, FF), BF16),
            pltpu.VMEM((NC, FF, CW), BF16),
            pltpu.VMEM((SEQ, 8, HEAD), BF16),
            pltpu.VMEM((SEQ, 8, HEAD), BF16),
            pltpu.VMEM((SEQ, 8, HEAD), BF16),
            pltpu.VMEM((SEQ, 8, HEAD), BF16),
            pltpu.VMEM(residual.shape, F32),
            pltpu.VMEM(residual.shape, BF16),
            pltpu.VMEM((YS, SUB, D // YS), BF16),
            pltpu.VMEM((ZS, SUB, 128), F32),
            pltpu.VMEM((2, HROWS, HALF * SUB), BF16),
            pltpu.VMEM((2, HALF * SUB, HROWS), BF16),
            pltpu.VMEM((2, HALF * SUB, HROWS), BF16),
            pltpu.VMEM((NC, ZS, SUB, CW), BF16),
            pltpu.VMEM((NC, 2, XS * CS, GROUP, CW), BF16),
            pltpu.VMEM((NC, 2, XS * CS, GROUP, CW), BF16),
            pltpu.VMEM((2, 2 * FF // TILE, HROWS, TILE), F32),
            pltpu.VMEM((2, HROWS, FF), BF16),
            pltpu.VMEM((NC, 2, XS * CS, GROUP, CW), BF16),
            pltpu.VMEM((NC, 2, XS * CS, GROUP, CW), BF16),
            pltpu.VMEM((NC, 2, HALF, SUB, CW), F32),
            pltpu.VMEM((NC, ZS - 1, SUB, CW), BF16),
            pltpu.VMEM((NC, ZS - 1, SUB, CW), BF16),
            pltpu.VMEM((NC, SUB, CW), BF16),
            pltpu.VMEM((YS, PER_Y, SUB, CW), BF16),
            dma((2,)), dma, dma, dma, dma,
            dma((ZS - 1,)), dma((ZS - 1,)),
            dma((YS - 1,)), dma((YS - 1,)),
            dma((NC, ZS - 1)), dma((NC, ZS - 1)),
            dma((NC, 2, peers)), dma((NC, 2, peers)),
            dma((2, NC, 2)),
            dma((NC, 2, peers)), dma((NC, 2, peers)),
            dma((NC, ZS - 1)), dma((NC, ZS - 1)),
            dma((NC,)), dma((NC,)),
        ],
        compiler_params=pltpu.CompilerParams(
            collective_id=0, has_side_effects=True, vmem_limit_bytes=60 * 1024 * 1024),
        name="layer",
    )(queries, key_vectors, value_vectors, residual, head_gain.reshape(1, -1), norm_gain.reshape(1, -1),
      routes.T, route_gates.T, expert_in, expert_out)


def solution(mesh):
    placed = (
        P("seq", "exp"), P("seq", "exp"), P("seq", "exp"), P("seq", "exp"), P("exp"), P(),
        P("seq", None), P("seq", None), P("seq", None, None, None), P("seq", None, None),
    )
    return jax.shard_map(
        per_device, mesh=mesh, in_specs=placed, out_specs=P("seq", "exp"), check_vma=False
    )
```

```python
import functools

import jax
import jax.numpy as jnp
from jax import lax
from jax.experimental import pallas as pl
from jax.experimental.pallas import tpu as pltpu
from jax.sharding import PartitionSpec as P

MESH = pl.DeviceIdType.MESH
F32 = jnp.float32
BF16 = jnp.bfloat16

HEAD = 128
XS, ZS, CS, YS = 4, 8, 2, 4
SEQ = XS * ZS * CS
D = 2048
FF = 1024
SUB = 32
CAP = 6
NC = 4
CW = D // NC
PER_Y = NC // YS
HALF = ZS // 2
GROUP = HALF * CAP
HROWS = XS * CS * GROUP
ROWS = 2 * HROWS
TILE = 256
PEERS = ((1, 0), (3, 0), (1, 1), (3, 1), (2, 0), (2, 1), (0, 1))
DIRECT = (True, True, False, False)
HOPS_RIGHT = (3, 3, 4, 3)
CHAIN_LEFT = {4: 3, 3: 2, 2: 1, 1: 0, 5: 6, 6: 7, 7: 0}
CHAIN_RIGHT = {4: 5, 5: 6, 6: 7, 7: 0, 3: 2, 2: 1, 1: 0}
SHORT_LEFT = {4: 3, 3: 0, 5: 6, 6: 0, 2: 0, 1: 0, 7: 0}
SHORT_RIGHT = {4: 5, 5: 6, 6: 0, 3: 0, 2: 0, 1: 0, 7: 0}
TREES = (CHAIN_LEFT, CHAIN_RIGHT, SHORT_RIGHT, SHORT_LEFT)
EARLY = 2


def nt(a, b):
    return lax.dot_general(a, b, (((1,), (1,)), ((), ())), preferred_element_type=F32)


def tn(a, b):
    return lax.dot_general(a, b, (((0,), (0,)), ((), ())), preferred_element_type=F32)


def nn(a, b):
    return jnp.dot(a, b, preferred_element_type=F32)


def halves(value):
    high = value.astype(BF16)
    return high, (value - high.astype(F32)).astype(BF16)


def layer_kernel(
    q_ref, k_ref, v_ref, res_ref, hgain_ref, ngain_ref, routes_ref, gates_ref, win_ref, wout_ref,
    out_ref,
    w1, w2, state, gathered, running, prior, raw, hidden, rows, meta, place, mixhi, mixlo,
    blk, sel, xin, acc, act, yout, ret, part, rs_send, rs_recv, mine, moe,
    w_sem, st_send, st_recv, pr_send, pr_recv, meta_send, meta_recv, y_send, y_recv,
    ag_send, ag_recv, xs_send, xs_recv, loc_sem, rt_send, rt_recv, rs_ssem, rs_rsem, fy_send, fy_recv,
):
    me = lax.axis_index("seq")
    y = lax.axis_index("exp")
    x = me // (ZS * CS)
    z = (me // CS) % ZS
    c = me % CS
    mine_d = x * CS + c

    def seq_id(xx, zz, cc):
        return (xx * ZS + zz) * CS + cc

    def remote(src, dst, ssem, rsem, seq=None, exp=None):
        return pltpu.make_async_remote_copy(
            src_ref=src, dst_ref=dst, send_sem=ssem, recv_sem=rsem,
            device_id=(me if seq is None else seq, y if exp is None else exp),
            device_id_type=MESH,
        )

    pending = []

    def go(copy):
        copy.start()
        pending.append(copy)
        return copy

    weights = []
    for q in range(NC):
        for g in range(2):
            weights.append(pltpu.make_async_copy(
                win_ref.at[0, g, pl.ds(q * CW, CW), :], w1.at[g, q], w_sem.at[0]))
    for q in range(NC):
        weights.append(pltpu.make_async_copy(
            wout_ref.at[0, :, pl.ds(q * CW, CW)], w2.at[q], w_sem.at[1]))
    for copy in weights:
        copy.start()

    barrier = pltpu.get_barrier_semaphore()

    def greet(i, _):
        pl.semaphore_signal(barrier, inc=1, device_id=((me + i) % SEQ, y), device_id_type=MESH)
        return 0

    lax.fori_loop(1, SEQ, greet, 0)
    for j in range(1, YS):
        pl.semaphore_signal(barrier, inc=1, device_id=(me, (y + j) % YS), device_id_type=MESH)

    heads = q_ref.shape[1] // HEAD
    for h in range(heads):
        cols = pl.ds(h * HEAD, HEAD)
        outer = tn(k_ref[:, cols], v_ref[:, cols])
        state[pl.ds(h * 16, 16)] = outer.reshape(16, 8, HEAD).astype(BF16)

    pl.semaphore_wait(barrier, SEQ - 1 + YS - 1)

    def send_state(i, _):
        for peer in ((me + i) % SEQ, (me + SEQ - i) % SEQ):
            remote(state.at[peer], gathered.at[me], st_send, st_recv, seq=peer).start()
        return 0

    lax.fori_loop(1, SEQ // 2, send_state, 0)
    far = (me + SEQ // 2) % SEQ
    remote(state.at[far], gathered.at[me], st_send, st_recv, seq=far).start()
    gathered[me] = state[me]

    tok = lax.broadcasted_iota(jnp.int32, (128, 128), 1)
    row = lax.broadcasted_iota(jnp.int32, (128, 128), 0)
    onehot = jnp.zeros((128, 128), F32)
    gate_rows = jnp.zeros((128, 128), F32)
    for k in range(routes_ref.shape[0]):
        route = routes_ref[k:k + 1, :]
        onehot = onehot + jnp.where(route == row, 1.0, 0.0)
        gate_rows = gate_rows + jnp.where(route + 64 == row, gates_ref[k:k + 1, :], 0.0)
    earlier = jnp.where((row < tok) & ((row >> 5) == (tok >> 5)), 1.0, 0.0).astype(BF16)
    table = onehot * (nn(onehot.astype(BF16), earlier) + 1.0) + gate_rows
    take = jnp.where(
        lax.broadcasted_iota(jnp.int32, (SUB, 128), 1) == lax.broadcasted_iota(jnp.int32, (SUB, 128), 0) + y * SUB,
        1.0, 0.0).astype(BF16)
    high, low = halves(table)
    meta[1] = nt(take, high) + nt(take, low)
    for k in range(1, ZS):
        go(remote(meta.at[1], meta.at[(k + 1) % ZS], meta_send.at[k - 1], meta_recv.at[k - 1],
                  seq=seq_id(x, (z + k) % ZS, c)))

    causal = row >= tok
    for h in range(heads):
        cols = pl.ds(h * HEAD, HEAD)
        scores = jnp.where(causal, nt(q_ref[:, cols], k_ref[:, cols]), 0.0)
        high, low = halves(scores)
        raw[:, cols] = nn(high, v_ref[:, cols]) + nn(low, v_ref[:, cols])

    def others(ref):
        return ref.at[pl.ds(0, SEQ - 1)]

    remote(others(state), others(gathered), st_send, st_recv).wait_recv()

    def scan_step(s, total):
        running[s] = total.astype(BF16)
        return total + gathered[s].astype(F32)

    lax.fori_loop(0, SEQ, scan_step, jnp.zeros((8, HEAD), F32))

    def send_prior(i, _):
        for peer in ((me + i) % SEQ, (me + SEQ - i) % SEQ):
            remote(running.at[peer], prior.at[me], pr_send, pr_recv, seq=peer).start()
        return 0

    lax.fori_loop(1, SEQ // 2, send_prior, 0)
    remote(running.at[far], prior.at[me], pr_send, pr_recv, seq=far).start()
    prior[me] = running[me]

    for copy in pending[:ZS - 1]:
        copy.wait_recv()
    everyone = meta[...].reshape(ZS * SUB, 128)
    meta_hi, meta_lo = halves(everyone)

    def slot_parts(shape, dim):
        index = lax.broadcasted_iota(jnp.int32, shape, dim)
        group = (index * 10923) >> 16
        return group >> 2, group & 3, index - group * CAP

    d_of, _, _ = slot_parts((HROWS, 128), 0)
    expert_of = seq_id(d_of >> 1, z, d_of & 1)
    lanes = lax.broadcasted_iota(jnp.int32, (HROWS, 128), 1)
    pick_rank = jnp.where(lanes == expert_of, 1.0, 0.0).astype(BF16)
    pick_gate = jnp.where(lanes == expert_of + 64, 1.0, 0.0).astype(BF16)
    _, k_row, r_row = slot_parts((HROWS, 128), 0)
    k_col = lanes >> 5
    _, mk_row, mr_row = slot_parts((128, HROWS), 1)
    mk_col = lax.broadcasted_iota(jnp.int32, (128, HROWS), 0) >> 5
    for hf in range(2):
        hi_part, lo_part = meta_hi[hf * 128:(hf + 1) * 128], meta_lo[hf * 128:(hf + 1) * 128]
        found = (nt(pick_rank, hi_part) == (r_row + 1).astype(F32)) & (k_row == k_col)
        place[hf] = jnp.where(found, 1.0, 0.0).astype(BF16)
        found = (nt(hi_part, pick_rank) == (mr_row + 1).astype(F32)) & (mk_row == mk_col)
        mix = jnp.where(found, nt(hi_part, pick_gate) + nt(lo_part, pick_gate), 0.0)
        high, low = halves(mix)
        mixhi[hf] = high
        mixlo[hf] = low

    remote(others(running), others(prior), pr_send, pr_recv).wait_recv()
    for h in range(heads):
        cols = pl.ds(h * HEAD, HEAD)
        before = prior[pl.ds(h * 16, 16)].astype(F32).reshape(HEAD, HEAD).astype(BF16)
        total = nn(q_ref[:, cols], before) + raw[:, cols]
        scale = lax.rsqrt(jnp.mean(total * total, axis=1, keepdims=True) + 1e-6)
        hidden[:, cols] = (res_ref[:, cols].astype(F32) + total * scale * hgain_ref[:, cols]).astype(BF16)

    y_copies = []
    for j in range(1, YS):
        peer = (y + j) % YS
        y_copies.append(go(remote(
            hidden.at[pl.ds(pl.multiple_of(peer * SUB, SUB), SUB), :], rows.at[y],
            y_send.at[j - 1], y_recv.at[j - 1], exp=peer)))
    rows[y] = hidden[pl.ds(pl.multiple_of(y * SUB, SUB), SUB), :]
    for copy in y_copies:
        copy.wait_recv()
    wide = [rows[j].astype(F32) for j in range(YS)]
    square = sum(jnp.sum(w * w, axis=1, keepdims=True) for w in wide)
    scale = lax.rsqrt(square * (1.0 / D) + 1e-6)
    for q in range(NC):
        part_cols = wide[q // PER_Y][:, (q % PER_Y) * CW:(q % PER_Y + 1) * CW]
        blk[q, 1] = (part_cols * scale * ngain_ref[:, q * CW:(q + 1) * CW]).astype(BF16)

    right = seq_id(x, (z + 1) % ZS, c)
    left = seq_id(x, (z + ZS - 1) % ZS, c)
    far_k = ZS // 2
    ag = {}

    def at(k):
        return (k + 1) % ZS

    def ag_right(q, k):
        ag["r", q, k] = go(remote(blk.at[q, at(k - 1)], blk.at[q, at(k)], ag_send.at[q, k - 1],
                                  ag_recv.at[q, k - 1], seq=right))

    def ag_left(q, k):
        ag["l", q, k] = go(remote(blk.at[q, at(ZS - k + 1)], blk.at[q, at(ZS - k)], ag_send.at[q, ZS - k - 1],
                                  ag_recv.at[q, ZS - k - 1], seq=left))

    def ag_begin(q):
        ag_right(q, 1)
        ag_left(q, 1)
        if DIRECT[q]:
            ag["r", q, 2] = go(remote(blk.at[q, at(0)], blk.at[q, at(2)], ag_send.at[q, 1], ag_recv.at[q, 1],
                                      seq=seq_id(x, (z + 2) % ZS, c)))

    def ag_from_left(q, k):
        if k <= HOPS_RIGHT[q]:
            ag["r", q, k].wait_recv()
            if k < HOPS_RIGHT[q] and not (DIRECT[q] and k == 1):
                ag_right(q, k + 1)

    def ag_from_right(q, k):
        hops = ZS - 1 - HOPS_RIGHT[q]
        if k <= hops:
            ag["l", q, k].wait_recv()
            if k < hops:
                ag_left(q, k + 1)

    xs = {}

    def select(q, hf):
        source = blk[q, hf * HALF:(hf + 1) * HALF].reshape(HALF * SUB, CW)
        sel[q, hf] = nn(place[hf], source).astype(BF16).reshape(XS * CS, GROUP, CW)
        for j, (dx, dc) in enumerate(PEERS):
            xx, cc = (x + dx) % XS, (c + dc) % CS
            xs[q, hf, j] = go(remote(sel.at[q, hf, xx * CS + cc], xin.at[q, hf, mine_d], xs_send.at[q, hf, j],
                                     xs_recv.at[q, hf, j], seq=seq_id(xx, z, cc)))
        own = pltpu.make_async_copy(sel.at[q, hf, mine_d], xin.at[q, hf, mine_d], loc_sem.at[0, q, hf])
        own.start()
        xs[q, hf, "own"] = own

    def expert_up(q, hf):
        if q == 0 and hf == 0:
            pltpu.make_async_copy(w1, w1, w_sem.at[0]).wait()
        for j in range(len(PEERS)):
            xs[q, hf, j].wait_recv()
        xs[q, hf, "own"].wait()

        def tile(i, _):
            cols = pl.ds(pl.multiple_of((i % 4) * TILE, TILE), TILE)
            value = nn(xin[q, hf].reshape(HROWS, CW), w1[i // 4, q, :, cols])
            if q == 0:
                acc[hf, i] = value
            else:
                acc[hf, i] += value
            return 0

        lax.fori_loop(0, 2 * FF // TILE, tile, 0, unroll=2)

    def activate(hf):
        for n in range(FF // TILE):
            gate = acc[hf, n]
            act[hf, :, n * TILE:(n + 1) * TILE] = (
                gate / (1.0 + jnp.exp(-gate)) * acc[hf, FF // TILE + n]).astype(BF16)

    rt = {}
    order = [(i + (y + 1) * PER_Y) % NC for i in range(NC)]

    def expert_down(i, hf):
        for n in range(CW // TILE):
            cols = pl.ds(n * TILE, TILE)
            value = nn(act[hf], w2[order[i], :, cols]).astype(BF16)
            yout[i, hf, :, :, cols] = value.reshape(XS * CS, GROUP, TILE)
        for j, (dx, dc) in enumerate(PEERS):
            xx, cc = (x + dx) % XS, (c + dc) % CS
            rt[i, hf, j] = go(remote(yout.at[i, hf, xx * CS + cc], ret.at[i, hf, mine_d], rt_send.at[i, hf, j],
                                     rt_recv.at[i, hf, j], seq=seq_id(xx, z, cc)))
        own = pltpu.make_async_copy(yout.at[i, hf, mine_d], ret.at[i, hf, mine_d], loc_sem.at[1, i, hf])
        own.start()
        rt[i, hf, "own"] = own

    for q in range(NC):
        ag_begin(q)
    for k in range(1, far_k + 1):
        for q in range(NC):
            if not (DIRECT[q] and k == 2):
                ag_from_left(q, k)
            ag_from_right(q, k)
            if DIRECT[q] and k == 1:
                ag_from_left(q, 2)
            if k == (1 if DIRECT[q] else 2):
                select(q, 0)
            if k == far_k:
                select(q, 1)
    for q in range(NC):
        expert_up(q, 0)
    activate(0)
    pltpu.make_async_copy(w2, w2, w_sem.at[1]).wait()
    for i in range(EARLY):
        expert_down(i, 0)
    for q in range(NC):
        expert_up(q, 1)
    activate(1)
    for i in range(NC):
        expert_down(i, 1)
    for i in range(EARLY, NC):
        expert_down(i, 0)

    rs = {}

    def answers(i, hf):
        for j in range(len(PEERS)):
            rt[i, hf, j].wait_recv()
        rt[i, hf, "own"].wait()
        value = ret[i, hf].reshape(HROWS, CW)
        part[i, hf] = (nn(mixhi[hf], value) + nn(mixlo[hf], value)).reshape(HALF, SUB, CW)

    def own_part(i, k):
        return part[i, at(k) // HALF, at(k) % HALF]

    def gathered_sum(i, k):
        total = own_part(i, k)
        for child, parent in TREES[i].items():
            if parent == k:
                rs[i, child].wait_recv()
                total = total + rs_recv[i, child - 1].astype(F32)
        return total.astype(BF16)

    def pass_on(i, k):
        rs_send[i, k - 1] = gathered_sum(i, k)
        target = seq_id(x, (z + TREES[i][k] - k + ZS) % ZS, c)
        rs[i, k] = go(remote(rs_send.at[i, k - 1], rs_recv.at[i, k - 1], rs_ssem.at[i, k - 1], rs_rsem.at[i, k - 1],
                             seq=target))

    def finish(i):
        total = gathered_sum(i, 0)
        if i < NC - PER_Y:
            mine[i] = total
            peer = (y + 1 + i // PER_Y) % YS
            rs["y", i] = go(remote(mine.at[i], moe.at[y, i % PER_Y], fy_send.at[i], fy_recv.at[i], exp=peer))
        else:
            moe[y, i % PER_Y] = total

    half_time, hop_time = 8.8, 2.8
    spacing = half_time / NC
    events = []
    for i in range(NC):
        far_at = half_time * EARLY / NC + spacing * (i + 1)
        near_at = spacing * (i + 1) if i < EARLY else half_time + spacing * (i + 1)
        events.append((near_at, i, 0, functools.partial(answers, i, 0)))
        events.append((far_at, i, 0, functools.partial(answers, i, 1)))
        sent_at = {}

        def ready(k):
            if k not in sent_at:
                held = near_at if k in (7, 0, 1, 2) else far_at
                waits = [ready(child) + hop_time for child, parent in TREES[i].items() if parent == k]
                sent_at[k] = max([held] + waits)
            return sent_at[k]

        for k in range(1, ZS):
            events.append((ready(k), i, 1, functools.partial(pass_on, i, k)))
        events.append((ready(0), i, 2, functools.partial(finish, i)))
    for event in sorted(events, key=lambda event: event[:3]):
        event[3]()

    for i in range(NC - PER_Y):
        rs["y", i].wait_recv()
    for j in range(YS):
        for p in range(PER_Y):
            cols = pl.ds(p * CW, CW)
            sub = pl.ds(j * SUB, SUB)
            out_ref[sub, cols] = (hidden[sub, cols].astype(F32) + moe[j, p].astype(F32)).astype(BF16)

    remote(others(state), others(gathered), st_send, st_recv).wait_send()
    remote(others(running), others(prior), pr_send, pr_recv).wait_send()
    for copy in pending:
        copy.wait_send()


def per_device(residual, queries, key_vectors, value_vectors, head_gain, norm_gain, routes, route_gates,
               expert_in, expert_out):
    vmem = pl.BlockSpec(memory_space=pltpu.VMEM)
    hbm = pl.BlockSpec(memory_space=pl.ANY)
    dma = pltpu.SemaphoreType.DMA
    peers = len(PEERS)
    return pl.pallas_call(
        layer_kernel,
        out_shape=jax.ShapeDtypeStruct(residual.shape, BF16),
        in_specs=[vmem] * 8 + [hbm] * 2,
        out_specs=vmem,
        scratch_shapes=[
            pltpu.VMEM((2, NC, CW, FF), BF16),
            pltpu.VMEM((NC, FF, CW), BF16),
            pltpu.VMEM((SEQ, 8, HEAD), BF16),
            pltpu.VMEM((SEQ, 8, HEAD), BF16),
            pltpu.VMEM((SEQ, 8, HEAD), BF16),
            pltpu.VMEM((SEQ, 8, HEAD), BF16),
            pltpu.VMEM(residual.shape, F32),
            pltpu.VMEM(residual.shape, BF16),
            pltpu.VMEM((YS, SUB, D // YS), BF16),
            pltpu.VMEM((ZS, SUB, 128), F32),
            pltpu.VMEM((2, HROWS, HALF * SUB), BF16),
            pltpu.VMEM((2, HALF * SUB, HROWS), BF16),
            pltpu.VMEM((2, HALF * SUB, HROWS), BF16),
            pltpu.VMEM((NC, ZS, SUB, CW), BF16),
            pltpu.VMEM((NC, 2, XS * CS, GROUP, CW), BF16),
            pltpu.VMEM((NC, 2, XS * CS, GROUP, CW), BF16),
            pltpu.VMEM((2, 2 * FF // TILE, HROWS, TILE), F32),
            pltpu.VMEM((2, HROWS, FF), BF16),
            pltpu.VMEM((NC, 2, XS * CS, GROUP, CW), BF16),
            pltpu.VMEM((NC, 2, XS * CS, GROUP, CW), BF16),
            pltpu.VMEM((NC, 2, HALF, SUB, CW), F32),
            pltpu.VMEM((NC, ZS - 1, SUB, CW), BF16),
            pltpu.VMEM((NC, ZS - 1, SUB, CW), BF16),
            pltpu.VMEM((NC, SUB, CW), BF16),
            pltpu.VMEM((YS, PER_Y, SUB, CW), BF16),
            dma((2,)), dma, dma, dma, dma,
            dma((ZS - 1,)), dma((ZS - 1,)),
            dma((YS - 1,)), dma((YS - 1,)),
            dma((NC, ZS - 1)), dma((NC, ZS - 1)),
            dma((NC, 2, peers)), dma((NC, 2, peers)),
            dma((2, NC, 2)),
            dma((NC, 2, peers)), dma((NC, 2, peers)),
            dma((NC, ZS - 1)), dma((NC, ZS - 1)),
            dma((NC,)), dma((NC,)),
        ],
        compiler_params=pltpu.CompilerParams(
            collective_id=0, has_side_effects=True, vmem_limit_bytes=60 * 1024 * 1024),
        name="layer",
    )(queries, key_vectors, value_vectors, residual, head_gain.reshape(1, -1), norm_gain.reshape(1, -1),
      routes.T, route_gates.T, expert_in, expert_out)


def solution(mesh):
    placed = (
        P("seq", "exp"), P("seq", "exp"), P("seq", "exp"), P("seq", "exp"), P("exp"), P(),
        P("seq", None), P("seq", None), P("seq", None, None, None), P("seq", None, None),
    )
    return jax.shard_map(
        per_device, mesh=mesh, in_specs=placed, out_specs=P("seq", "exp"), check_vma=False
    )
```

```python
import functools

import jax
import jax.numpy as jnp
from jax import lax
from jax.experimental import pallas as pl
from jax.experimental.pallas import tpu as pltpu
from jax.sharding import PartitionSpec as P

MESH = pl.DeviceIdType.MESH
F32 = jnp.float32
BF16 = jnp.bfloat16

HEAD = 128
XS, ZS, CS, YS = 4, 8, 2, 4
SEQ = XS * ZS * CS
SLAB = ZS * CS
PIECE = 512 // SLAB
D = 2048
FF = 1024
SUB = 32
CAP = 6
NC = 4
CW = D // NC
PER_Y = NC // YS
HALF = ZS // 2
GROUP = HALF * CAP
HROWS = XS * CS * GROUP
ROWS = 2 * HROWS
TILE = 256
PEERS = ((1, 0), (3, 0), (1, 1), (3, 1), (2, 0), (2, 1), (0, 1))


def nt(a, b):
    return lax.dot_general(a, b, (((1,), (1,)), ((), ())), preferred_element_type=F32)


def tn(a, b):
    return lax.dot_general(a, b, (((0,), (0,)), ((), ())), preferred_element_type=F32)


def nn(a, b):
    return jnp.dot(a, b, preferred_element_type=F32)


def halves(value):
    high = value.astype(BF16)
    return high, (value - high.astype(F32)).astype(BF16)


def layer_kernel(
    q_ref, k_ref, v_ref, res_ref, hgain_ref, ngain_ref, routes_ref, gates_ref, win_ref, wout_ref,
    out_ref,
    w1, w2, state, gathered, running, prior, totals, raw, hidden, rows, meta, place, mixhi, mixlo,
    blk, sel, xin, acc, act, yout, ret, part, rs_send, rs_recv, mine, moe,
    w_sem, st_send, st_recv, tot_send, tot_recv, pr_send, pr_recv, meta_send, meta_recv, y_send, y_recv,
    ag_send, ag_recv, xs_send, xs_recv, loc_sem, rt_send, rt_recv, rs_ssem, rs_rsem, fy_send, fy_recv,
):
    me = lax.axis_index("seq")
    y = lax.axis_index("exp")
    x = me // (ZS * CS)
    z = (me // CS) % ZS
    c = me % CS
    mine_d = x * CS + c

    def seq_id(xx, zz, cc):
        return (xx * ZS + zz) * CS + cc

    def remote(src, dst, ssem, rsem, seq=None, exp=None):
        return pltpu.make_async_remote_copy(
            src_ref=src, dst_ref=dst, send_sem=ssem, recv_sem=rsem,
            device_id=(me if seq is None else seq, y if exp is None else exp),
            device_id_type=MESH,
        )

    pending = []

    def go(copy):
        copy.start()
        pending.append(copy)
        return copy

    weights = []
    for q in range(NC):
        for g in range(2):
            weights.append(pltpu.make_async_copy(
                win_ref.at[0, g, pl.ds(q * CW, CW), :], w1.at[g, q], w_sem.at[0]))
    for q in range(NC):
        weights.append(pltpu.make_async_copy(
            wout_ref.at[0, :, pl.ds(q * CW, CW)], w2.at[q], w_sem.at[1]))
    for copy in weights:
        copy.start()

    barrier = pltpu.get_barrier_semaphore()

    place_in_slab = me % SLAB
    shifts = [SLAB // 2] + [shift for i in range(SLAB // 2 - 1, 0, -1) for shift in (i, SLAB - i)]
    slab_peers = [(x * SLAB + (place_in_slab + shift) % SLAB, (place_in_slab + shift) % SLAB) for shift in shifts]

    def greet(peer, other=None):
        pl.semaphore_signal(barrier, inc=1, device_id=(peer, y if other is None else other), device_id_type=MESH)

    for peer, _ in slab_peers:
        greet(peer)
    for dx, dc in PEERS:
        if dx:
            greet(seq_id((x + dx) % XS, z, (c + dc) % CS))
    for j in range(1, YS):
        greet(me, (y + j) % YS)
    greeted = SLAB - 1 + (XS - 1) * CS + YS - 1

    heads = q_ref.shape[1] // HEAD
    for h in range(heads):
        cols = pl.ds(h * HEAD, HEAD)
        outer = tn(k_ref[:, cols], v_ref[:, cols])
        state[pl.ds(h * HEAD // PIECE, HEAD // PIECE)] = outer.reshape(HEAD // PIECE, PIECE, HEAD).astype(BF16)

    pl.semaphore_wait(barrier, greeted)
    for peer, where in slab_peers:
        remote(state.at[where], gathered.at[place_in_slab], st_send, st_recv, seq=peer).start()
    gathered[place_in_slab] = state[place_in_slab]

    tok = lax.broadcasted_iota(jnp.int32, (128, 128), 1)
    row = lax.broadcasted_iota(jnp.int32, (128, 128), 0)
    onehot = jnp.zeros((128, 128), F32)
    gate_rows = jnp.zeros((128, 128), F32)
    for k in range(routes_ref.shape[0]):
        route = routes_ref[k:k + 1, :]
        onehot = onehot + jnp.where(route == row, 1.0, 0.0)
        gate_rows = gate_rows + jnp.where(route + 64 == row, gates_ref[k:k + 1, :], 0.0)
    earlier = jnp.where((row < tok) & ((row >> 5) == (tok >> 5)), 1.0, 0.0).astype(BF16)
    table = onehot * (nn(onehot.astype(BF16), earlier) + 1.0) + gate_rows
    take = jnp.where(
        lax.broadcasted_iota(jnp.int32, (SUB, 128), 1) == lax.broadcasted_iota(jnp.int32, (SUB, 128), 0) + y * SUB,
        1.0, 0.0).astype(BF16)
    high, low = halves(table)
    meta[1] = nt(take, high) + nt(take, low)
    for k in range(1, ZS):
        go(remote(meta.at[1], meta.at[(k + 1) % ZS], meta_send.at[k - 1], meta_recv.at[k - 1],
                  seq=seq_id(x, (z + k) % ZS, c)))

    causal = row >= tok
    for h in range(heads):
        cols = pl.ds(h * HEAD, HEAD)
        scores = jnp.where(causal, nt(q_ref[:, cols], k_ref[:, cols]), 0.0)
        high, low = halves(scores)
        raw[:, cols] = nn(high, v_ref[:, cols]) + nn(low, v_ref[:, cols])

    def others(ref):
        return ref.at[pl.ds(0, SLAB - 1)]

    remote(others(state), others(gathered), st_send, st_recv).wait_recv()

    total = jnp.zeros((PIECE, HEAD), F32)
    for g in range(SLAB):
        total = total + gathered[g].astype(F32)
    totals[x] = total
    slab_copies = []
    for dx in (2, 1, 3):
        slab_copies.append(go(remote(totals.at[x], totals.at[x], tot_send.at[dx - 1], tot_recv.at[dx - 1],
                                     seq=seq_id((x + dx) % XS, z, c))))
    for copy in slab_copies:
        copy.wait_recv()
    total = jnp.zeros((PIECE, HEAD), F32)
    for xx in range(XS):
        total = total + jnp.where(xx < x, totals[xx], 0.0)
    for g in range(SLAB):
        running[g] = total.astype(BF16)
        total = total + gathered[g].astype(F32)
    for peer, where in slab_peers:
        remote(running.at[where], prior.at[place_in_slab], pr_send, pr_recv, seq=peer).start()
    prior[place_in_slab] = running[place_in_slab]

    for copy in pending[:ZS - 1]:
        copy.wait_recv()
    everyone = meta[...].reshape(ZS * SUB, 128)
    meta_hi, meta_lo = halves(everyone)

    def slot_parts(shape, dim):
        index = lax.broadcasted_iota(jnp.int32, shape, dim)
        group = (index * 10923) >> 16
        return group >> 2, group & 3, index - group * CAP

    d_of, _, _ = slot_parts((HROWS, 128), 0)
    expert_of = seq_id(d_of >> 1, z, d_of & 1)
    lanes = lax.broadcasted_iota(jnp.int32, (HROWS, 128), 1)
    pick_rank = jnp.where(lanes == expert_of, 1.0, 0.0).astype(BF16)
    pick_gate = jnp.where(lanes == expert_of + 64, 1.0, 0.0).astype(BF16)
    _, k_row, r_row = slot_parts((HROWS, 128), 0)
    k_col = lanes >> 5
    _, mk_row, mr_row = slot_parts((128, HROWS), 1)
    mk_col = lax.broadcasted_iota(jnp.int32, (128, HROWS), 0) >> 5
    for hf in range(2):
        hi_part, lo_part = meta_hi[hf * 128:(hf + 1) * 128], meta_lo[hf * 128:(hf + 1) * 128]
        found = (nt(pick_rank, hi_part) == (r_row + 1).astype(F32)) & (k_row == k_col)
        place[hf] = jnp.where(found, 1.0, 0.0).astype(BF16)
        found = (nt(hi_part, pick_rank) == (mr_row + 1).astype(F32)) & (mk_row == mk_col)
        mix = jnp.where(found, nt(hi_part, pick_gate) + nt(lo_part, pick_gate), 0.0)
        high, low = halves(mix)
        mixhi[hf] = high
        mixlo[hf] = low

    remote(others(running), others(prior), pr_send, pr_recv).wait_recv()
    for h in range(heads):
        cols = pl.ds(h * HEAD, HEAD)
        before = prior[pl.ds(h * HEAD // PIECE, HEAD // PIECE)].reshape(HEAD, HEAD)
        total = nn(q_ref[:, cols], before) + raw[:, cols]
        scale = lax.rsqrt(jnp.mean(total * total, axis=1, keepdims=True) + 1e-6)
        hidden[:, cols] = (res_ref[:, cols].astype(F32) + total * scale * hgain_ref[:, cols]).astype(BF16)

    y_copies = []
    for j in range(1, YS):
        peer = (y + j) % YS
        y_copies.append(go(remote(
            hidden.at[pl.ds(pl.multiple_of(peer * SUB, SUB), SUB), :], rows.at[y],
            y_send.at[j - 1], y_recv.at[j - 1], exp=peer)))
    rows[y] = hidden[pl.ds(pl.multiple_of(y * SUB, SUB), SUB), :]
    for copy in y_copies:
        copy.wait_recv()
    wide = [rows[j].astype(F32) for j in range(YS)]
    square = sum(jnp.sum(w * w, axis=1, keepdims=True) for w in wide)
    scale = lax.rsqrt(square * (1.0 / D) + 1e-6)
    for q in range(NC):
        part_cols = wide[q // PER_Y][:, (q % PER_Y) * CW:(q % PER_Y + 1) * CW]
        blk[q, 1] = (part_cols * scale * ngain_ref[:, q * CW:(q + 1) * CW]).astype(BF16)

    right = seq_id(x, (z + 1) % ZS, c)
    left = seq_id(x, (z + ZS - 1) % ZS, c)
    far_k = ZS // 2
    ag = {}

    def at(k):
        return (k + 1) % ZS

    def ag_right(q, k):
        ag["r", q, k] = go(remote(blk.at[q, at(k - 1)], blk.at[q, at(k)], ag_send.at[q, k - 1],
                                  ag_recv.at[q, k - 1], seq=right))

    def ag_left(q, k):
        ag["l", q, k] = go(remote(blk.at[q, at(ZS - k + 1)], blk.at[q, at(ZS - k)], ag_send.at[q, ZS - k - 1],
                                  ag_recv.at[q, ZS - k - 1], seq=left))

    def ag_step(q, k):
        if k > 0:
            ag["r", q, k].wait_recv()
        if k < far_k:
            ag_right(q, k + 1)
        if 0 < k < far_k:
            ag["l", q, k].wait_recv()
        if k + 1 < far_k:
            ag_left(q, k + 1)

    xs = {}

    def select(q, hf):
        source = blk[q, hf * HALF:(hf + 1) * HALF].reshape(HALF * SUB, CW)
        sel[q, hf] = nn(place[hf], source).astype(BF16).reshape(XS * CS, GROUP, CW)
        for j, (dx, dc) in enumerate(PEERS):
            xx, cc = (x + dx) % XS, (c + dc) % CS
            xs[q, hf, j] = go(remote(sel.at[q, hf, xx * CS + cc], xin.at[q, hf, mine_d], xs_send.at[q, hf, j],
                                     xs_recv.at[q, hf, j], seq=seq_id(xx, z, cc)))
        own = pltpu.make_async_copy(sel.at[q, hf, mine_d], xin.at[q, hf, mine_d], loc_sem.at[0, q, hf])
        own.start()
        xs[q, hf, "own"] = own

    def expert_up(q, hf):
        if q == 0 and hf == 0:
            pltpu.make_async_copy(w1, w1, w_sem.at[0]).wait()
        for j in range(len(PEERS)):
            xs[q, hf, j].wait_recv()
        xs[q, hf, "own"].wait()

        def tile(i, _):
            cols = pl.ds(pl.multiple_of((i % 4) * TILE, TILE), TILE)
            value = nn(xin[q, hf].reshape(HROWS, CW), w1[i // 4, q, :, cols])
            if q == 0:
                acc[hf, i] = value
            else:
                acc[hf, i] += value
            return 0

        lax.fori_loop(0, 2 * FF // TILE, tile, 0, unroll=2)

    def activate(hf):
        for n in range(FF // TILE):
            gate = acc[hf, n]
            act[hf, :, n * TILE:(n + 1) * TILE] = (
                gate / (1.0 + jnp.exp(-gate)) * acc[hf, FF // TILE + n]).astype(BF16)

    rt = {}
    order = [(i + (y + 1) * PER_Y) % NC for i in range(NC)]

    def expert_down(i, hf):
        for n in range(CW // TILE):
            cols = pl.ds(n * TILE, TILE)
            value = nn(act[hf], w2[order[i], :, cols]).astype(BF16)
            yout[i, hf, :, :, cols] = value.reshape(XS * CS, GROUP, TILE)
        for j, (dx, dc) in enumerate(PEERS):
            xx, cc = (x + dx) % XS, (c + dc) % CS
            rt[i, hf, j] = go(remote(yout.at[i, hf, xx * CS + cc], ret.at[i, hf, mine_d], rt_send.at[i, hf, j],
                                     rt_recv.at[i, hf, j], seq=seq_id(xx, z, cc)))
        own = pltpu.make_async_copy(yout.at[i, hf, mine_d], ret.at[i, hf, mine_d], loc_sem.at[1, i, hf])
        own.start()
        rt[i, hf, "own"] = own

    for q in range(NC):
        ag_step(q, 0)
    for k in range(1, far_k + 1):
        for q in range(NC):
            ag_step(q, k)
            if k == 2:
                select(q, 0)
            if k == far_k:
                select(q, 1)
    for q in range(NC):
        expert_up(q, 0)
    activate(0)
    pltpu.make_async_copy(w2, w2, w_sem.at[1]).wait()
    for i in range(NC // 2):
        expert_down(i, 0)
    for q in range(NC):
        expert_up(q, 1)
    activate(1)
    for i in range(NC):
        expert_down(i, 1)
    for i in range(NC // 2, NC):
        expert_down(i, 0)

    rs = {}

    def answers(i, hf):
        for j in range(len(PEERS)):
            rt[i, hf, j].wait_recv()
        rt[i, hf, "own"].wait()
        value = ret[i, hf].reshape(HROWS, CW)
        part[i, hf] = (nn(mixhi[hf], value) + nn(mixlo[hf], value)).reshape(HALF, SUB, CW)

    def own_part(i, k):
        return part[i, at(k) // HALF, at(k) % HALF]

    def send_sum(i, slot, value, shift):
        rs_send[i, slot] = value.astype(BF16)
        rs[i, slot] = go(remote(rs_send.at[i, slot], rs_recv.at[i, slot], rs_ssem.at[i, slot], rs_rsem.at[i, slot],
                                seq=seq_id(x, (z + shift) % ZS, c)))

    def far_rows(i):
        answers(i, 1)
        send_sum(i, 0, own_part(i, 4), ZS - 1)
        send_sum(i, 1, own_part(i, 5), 1)

    def far_sums(i):
        rs[i, 0].wait_recv()
        send_sum(i, 2, own_part(i, 3) + rs_recv[i, 0].astype(F32), ZS - 3)
        rs[i, 1].wait_recv()
        send_sum(i, 3, own_part(i, 6) + rs_recv[i, 1].astype(F32), 2)

    def near_rows(i):
        answers(i, 0)
        send_sum(i, 4, own_part(i, 2), ZS - 2)
        send_sum(i, 5, own_part(i, 1), ZS - 1)
        send_sum(i, 6, own_part(i, 7), 1)

    def finish(i):
        total = own_part(i, 0)
        for slot in range(2, ZS - 1):
            rs[i, slot].wait_recv()
            total = total + rs_recv[i, slot].astype(F32)
        total = total.astype(BF16)
        if i < NC - PER_Y:
            mine[i] = total
            peer = (y + 1 + i // PER_Y) % YS
            rs["y", i] = go(remote(mine.at[i], moe.at[y, i % PER_Y], fy_send.at[i], fy_recv.at[i], exp=peer))
        else:
            moe[y, i % PER_Y] = total

    half_time = 8.8
    spacing = half_time / NC
    events = []
    for i in range(NC):
        far_at = half_time / 2 + spacing * (i + 1)
        near_at = spacing * (i + 1) if i < NC // 2 else half_time + spacing * (i + 1)
        events.append((near_at, i, near_rows))
        events.append((far_at, i, far_rows))
        events.append((far_at + 2.8, i, far_sums))
        events.append((max(far_at + 6.7, near_at + 3.2), i, finish))
    for when, i, act_on in sorted(events, key=lambda event: event[:2]):
        act_on(i)

    for i in range(NC - PER_Y):
        rs["y", i].wait_recv()
    for j in range(YS):
        for p in range(PER_Y):
            cols = pl.ds(p * CW, CW)
            sub = pl.ds(j * SUB, SUB)
            out_ref[sub, cols] = (hidden[sub, cols].astype(F32) + moe[j, p].astype(F32)).astype(BF16)

    remote(others(state), others(gathered), st_send, st_recv).wait_send()
    remote(others(running), others(prior), pr_send, pr_recv).wait_send()
    for copy in pending:
        copy.wait_send()


def per_device(residual, queries, key_vectors, value_vectors, head_gain, norm_gain, routes, route_gates,
               expert_in, expert_out):
    vmem = pl.BlockSpec(memory_space=pltpu.VMEM)
    hbm = pl.BlockSpec(memory_space=pl.ANY)
    dma = pltpu.SemaphoreType.DMA
    peers = len(PEERS)
    return pl.pallas_call(
        layer_kernel,
        out_shape=jax.ShapeDtypeStruct(residual.shape, BF16),
        in_specs=[vmem] * 8 + [hbm] * 2,
        out_specs=vmem,
        scratch_shapes=[
            pltpu.VMEM((2, NC, CW, FF), BF16),
            pltpu.VMEM((NC, FF, CW), BF16),
            pltpu.VMEM((SLAB, PIECE, HEAD), BF16),
            pltpu.VMEM((SLAB, PIECE, HEAD), BF16),
            pltpu.VMEM((SLAB, PIECE, HEAD), BF16),
            pltpu.VMEM((SLAB, PIECE, HEAD), BF16),
            pltpu.VMEM((XS, PIECE, HEAD), F32),
            pltpu.VMEM(residual.shape, F32),
            pltpu.VMEM(residual.shape, BF16),
            pltpu.VMEM((YS, SUB, D // YS), BF16),
            pltpu.VMEM((ZS, SUB, 128), F32),
            pltpu.VMEM((2, HROWS, HALF * SUB), BF16),
            pltpu.VMEM((2, HALF * SUB, HROWS), BF16),
            pltpu.VMEM((2, HALF * SUB, HROWS), BF16),
            pltpu.VMEM((NC, ZS, SUB, CW), BF16),
            pltpu.VMEM((NC, 2, XS * CS, GROUP, CW), BF16),
            pltpu.VMEM((NC, 2, XS * CS, GROUP, CW), BF16),
            pltpu.VMEM((2, 2 * FF // TILE, HROWS, TILE), F32),
            pltpu.VMEM((2, HROWS, FF), BF16),
            pltpu.VMEM((NC, 2, XS * CS, GROUP, CW), BF16),
            pltpu.VMEM((NC, 2, XS * CS, GROUP, CW), BF16),
            pltpu.VMEM((NC, 2, HALF, SUB, CW), F32),
            pltpu.VMEM((NC, ZS - 1, SUB, CW), BF16),
            pltpu.VMEM((NC, ZS - 1, SUB, CW), BF16),
            pltpu.VMEM((NC, SUB, CW), BF16),
            pltpu.VMEM((YS, PER_Y, SUB, CW), BF16),
            dma((2,)), dma, dma, dma((XS - 1,)), dma((XS - 1,)), dma, dma,
            dma((ZS - 1,)), dma((ZS - 1,)),
            dma((YS - 1,)), dma((YS - 1,)),
            dma((NC, ZS - 1)), dma((NC, ZS - 1)),
            dma((NC, 2, peers)), dma((NC, 2, peers)),
            dma((2, NC, 2)),
            dma((NC, 2, peers)), dma((NC, 2, peers)),
            dma((NC, ZS - 1)), dma((NC, ZS - 1)),
            dma((NC,)), dma((NC,)),
        ],
        compiler_params=pltpu.CompilerParams(
            collective_id=0, has_side_effects=True, vmem_limit_bytes=60 * 1024 * 1024),
        name="layer",
    )(queries, key_vectors, value_vectors, residual, head_gain.reshape(1, -1), norm_gain.reshape(1, -1),
      routes.T, route_gates.T, expert_in, expert_out)


def solution(mesh):
    placed = (
        P("seq", "exp"), P("seq", "exp"), P("seq", "exp"), P("seq", "exp"), P("exp"), P(),
        P("seq", None), P("seq", None), P("seq", None, None, None), P("seq", None, None),
    )
    return jax.shard_map(
        per_device, mesh=mesh, in_specs=placed, out_specs=P("seq", "exp"), check_vma=False
    )
```

```python
import functools

import jax
import jax.numpy as jnp
from jax import lax
from jax.experimental import pallas as pl
from jax.experimental.pallas import tpu as pltpu
from jax.sharding import PartitionSpec as P

MESH = pl.DeviceIdType.MESH
F32 = jnp.float32
BF16 = jnp.bfloat16

HEAD = 128
XS, ZS, CS, YS = 4, 8, 2, 4
SEQ = XS * ZS * CS
SLAB = ZS * CS
PIECE = 512 // SLAB
D = 2048
FF = 1024
SUB = 32
CAP = 6
NC = 4
CW = D // NC
PER_Y = NC // YS
HALF = ZS // 2
GROUP = HALF * CAP
HROWS = XS * CS * GROUP
ROWS = 2 * HROWS
TILE = 256
PEERS = ((1, 0), (3, 0), (1, 1), (3, 1), (2, 0), (2, 1), (0, 1))
HOPS_RIGHT = (4, 3, 4, 3)
SHORT_LEFT = {4: 3, 3: 0, 5: 6, 6: 0, 2: 0, 1: 0, 7: 0}
TREES = (SHORT_LEFT,) * 4
PIECES = ((0, 0), (1, 0), (0, 1), (1, 1), (2, 1), (3, 1), (2, 0), (3, 0))
EARLY = 2
WINDOW = 4


def nt(a, b):
    return lax.dot_general(a, b, (((1,), (1,)), ((), ())), preferred_element_type=F32)


def tn(a, b):
    return lax.dot_general(a, b, (((0,), (0,)), ((), ())), preferred_element_type=F32)


def nn(a, b):
    return jnp.dot(a, b, preferred_element_type=F32)


def halves(value):
    high = value.astype(BF16)
    return high, (value - high.astype(F32)).astype(BF16)


def layer_kernel(
    q_ref, k_ref, v_ref, res_ref, hgain_ref, ngain_ref, routes_ref, gates_ref, win_ref, wout_ref,
    out_ref,
    w1, w2, state, gathered, running, prior, totals, raw, hidden, rows, meta, place, mixhi, mixlo,
    blk, sel, xin, acc, act, yout, ret, part, rs_send, rs_recv, mine, moe,
    w_sem, st_send, st_recv, tot_send, tot_recv, pr_send, pr_recv, meta_send, meta_recv, y_send, y_recv,
    ag_send, ag_recv, xs_send, xs_recv, loc_sem, rt_send, rt_recv, rs_ssem, rs_rsem, fy_send, fy_recv,
):
    me = lax.axis_index("seq")
    y = lax.axis_index("exp")
    x = me // (ZS * CS)
    z = (me // CS) % ZS
    c = me % CS
    mine_d = x * CS + c

    def seq_id(xx, zz, cc):
        return (xx * ZS + zz) * CS + cc

    def remote(src, dst, ssem, rsem, seq=None, exp=None):
        return pltpu.make_async_remote_copy(
            src_ref=src, dst_ref=dst, send_sem=ssem, recv_sem=rsem,
            device_id=(me if seq is None else seq, y if exp is None else exp),
            device_id_type=MESH,
        )

    pending = []

    def go(copy):
        copy.start()
        pending.append(copy)
        return copy

    weights = []
    for q in range(NC):
        for g in range(2):
            weights.append(pltpu.make_async_copy(
                win_ref.at[0, g, pl.ds(q * CW, CW), :], w1.at[g, q], w_sem.at[0]))
    for q in range(NC):
        weights.append(pltpu.make_async_copy(
            wout_ref.at[0, :, pl.ds(q * CW, CW)], w2.at[q], w_sem.at[1]))
    for copy in weights:
        copy.start()

    barrier = pltpu.get_barrier_semaphore()

    place_in_slab = me % SLAB
    shifts = [SLAB // 2] + [shift for i in range(SLAB // 2 - 1, 0, -1) for shift in (i, SLAB - i)]
    slab_peers = [(x * SLAB + (place_in_slab + shift) % SLAB, (place_in_slab + shift) % SLAB) for shift in shifts]

    def greet(peer, other=None):
        pl.semaphore_signal(barrier, inc=1, device_id=(peer, y if other is None else other), device_id_type=MESH)

    for peer, _ in slab_peers:
        greet(peer)
    for dx, dc in PEERS:
        if dx:
            greet(seq_id((x + dx) % XS, z, (c + dc) % CS))
    for j in range(1, YS):
        greet(me, (y + j) % YS)
    greeted = SLAB - 1 + (XS - 1) * CS + YS - 1

    heads = q_ref.shape[1] // HEAD
    for h in range(heads):
        cols = pl.ds(h * HEAD, HEAD)
        outer = tn(k_ref[:, cols], v_ref[:, cols])
        state[pl.ds(h * HEAD // PIECE, HEAD // PIECE)] = outer.reshape(HEAD // PIECE, PIECE, HEAD).astype(BF16)

    pl.semaphore_wait(barrier, greeted)
    for peer, where in slab_peers:
        remote(state.at[where], gathered.at[place_in_slab], st_send, st_recv, seq=peer).start()
    gathered[place_in_slab] = state[place_in_slab]

    tok = lax.broadcasted_iota(jnp.int32, (128, 128), 1)
    row = lax.broadcasted_iota(jnp.int32, (128, 128), 0)
    onehot = jnp.zeros((128, 128), F32)
    gate_rows = jnp.zeros((128, 128), F32)
    for k in range(routes_ref.shape[0]):
        route = routes_ref[k:k + 1, :]
        onehot = onehot + jnp.where(route == row, 1.0, 0.0)
        gate_rows = gate_rows + jnp.where(route + 64 == row, gates_ref[k:k + 1, :], 0.0)
    earlier = jnp.where((row < tok) & ((row >> 5) == (tok >> 5)), 1.0, 0.0).astype(BF16)
    table = onehot * (nn(onehot.astype(BF16), earlier) + 1.0) + gate_rows
    take = jnp.where(
        lax.broadcasted_iota(jnp.int32, (SUB, 128), 1) == lax.broadcasted_iota(jnp.int32, (SUB, 128), 0) + y * SUB,
        1.0, 0.0).astype(BF16)
    high, low = halves(table)
    meta[1] = nt(take, high) + nt(take, low)
    for k in range(1, ZS):
        go(remote(meta.at[1], meta.at[(k + 1) % ZS], meta_send.at[k - 1], meta_recv.at[k - 1],
                  seq=seq_id(x, (z + k) % ZS, c)))

    causal = row >= tok
    for h in range(heads):
        cols = pl.ds(h * HEAD, HEAD)
        scores = jnp.where(causal, nt(q_ref[:, cols], k_ref[:, cols]), 0.0)
        high, low = halves(scores)
        raw[:, cols] = nn(high, v_ref[:, cols]) + nn(low, v_ref[:, cols])

    def others(ref):
        return ref.at[pl.ds(0, SLAB - 1)]

    remote(others(state), others(gathered), st_send, st_recv).wait_recv()

    total = jnp.zeros((PIECE, HEAD), F32)
    for g in range(SLAB):
        total = total + gathered[g].astype(F32)
    totals[x] = total
    slab_copies = []
    for dx in (2, 1, 3):
        slab_copies.append(go(remote(totals.at[x], totals.at[x], tot_send.at[dx - 1], tot_recv.at[dx - 1],
                                     seq=seq_id((x + dx) % XS, z, c))))
    for copy in slab_copies:
        copy.wait_recv()
    total = jnp.zeros((PIECE, HEAD), F32)
    for xx in range(XS):
        total = total + jnp.where(xx < x, totals[xx], 0.0)
    for g in range(SLAB):
        running[g] = total.astype(BF16)
        total = total + gathered[g].astype(F32)
    for peer, where in slab_peers:
        remote(running.at[where], prior.at[place_in_slab], pr_send, pr_recv, seq=peer).start()
    prior[place_in_slab] = running[place_in_slab]

    for copy in pending[:ZS - 1]:
        copy.wait_recv()
    everyone = meta[...].reshape(ZS * SUB, 128)
    meta_hi, meta_lo = halves(everyone)

    def slot_parts(shape, dim):
        index = lax.broadcasted_iota(jnp.int32, shape, dim)
        group = (index * 10923) >> 16
        return group >> 2, group & 3, index - group * CAP

    d_of, _, _ = slot_parts((HROWS, 128), 0)
    expert_of = seq_id(d_of >> 1, z, d_of & 1)
    lanes = lax.broadcasted_iota(jnp.int32, (HROWS, 128), 1)
    pick_rank = jnp.where(lanes == expert_of, 1.0, 0.0).astype(BF16)
    pick_gate = jnp.where(lanes == expert_of + 64, 1.0, 0.0).astype(BF16)
    _, k_row, r_row = slot_parts((HROWS, 128), 0)
    k_col = lanes >> 5
    _, mk_row, mr_row = slot_parts((128, HROWS), 1)
    mk_col = lax.broadcasted_iota(jnp.int32, (128, HROWS), 0) >> 5
    for hf in range(2):
        hi_part, lo_part = meta_hi[hf * 128:(hf + 1) * 128], meta_lo[hf * 128:(hf + 1) * 128]
        found = (nt(pick_rank, hi_part) == (r_row + 1).astype(F32)) & (k_row == k_col)
        place[hf] = jnp.where(found, 1.0, 0.0).astype(BF16)
        found = (nt(hi_part, pick_rank) == (mr_row + 1).astype(F32)) & (mk_row == mk_col)
        mix = jnp.where(found, nt(hi_part, pick_gate) + nt(lo_part, pick_gate), 0.0)
        high, low = halves(mix)
        mixhi[hf] = high
        mixlo[hf] = low

    remote(others(running), others(prior), pr_send, pr_recv).wait_recv()
    for h in range(heads):
        cols = pl.ds(h * HEAD, HEAD)
        before = prior[pl.ds(h * HEAD // PIECE, HEAD // PIECE)].reshape(HEAD, HEAD)
        total = nn(q_ref[:, cols], before) + raw[:, cols]
        scale = lax.rsqrt(jnp.mean(total * total, axis=1, keepdims=True) + 1e-6)
        hidden[:, cols] = (res_ref[:, cols].astype(F32) + total * scale * hgain_ref[:, cols]).astype(BF16)

    y_copies = []
    for j in range(1, YS):
        peer = (y + j) % YS
        y_copies.append(go(remote(
            hidden.at[pl.ds(pl.multiple_of(peer * SUB, SUB), SUB), :], rows.at[y],
            y_send.at[j - 1], y_recv.at[j - 1], exp=peer)))
    rows[y] = hidden[pl.ds(pl.multiple_of(y * SUB, SUB), SUB), :]
    right = seq_id(x, (z + 1) % ZS, c)
    left = seq_id(x, (z + ZS - 1) % ZS, c)
    far_k = ZS // 2
    ag = {}

    def at(k):
        return (k + 1) % ZS

    def ag_right(q, k):
        ag["r", q, k] = go(remote(blk.at[q, at(k - 1)], blk.at[q, at(k)], ag_send.at[q, k - 1],
                                  ag_recv.at[q, k - 1], seq=right))

    def ag_left(q, k):
        ag["l", q, k] = go(remote(blk.at[q, at(ZS - k + 1)], blk.at[q, at(ZS - k)], ag_send.at[q, ZS - k - 1],
                                  ag_recv.at[q, ZS - k - 1], seq=left))

    def ag_begin(q):
        ag_right(q, 1)
        ag_left(q, 1)

    for copy in y_copies:
        copy.wait_recv()
    wide = [rows[j].astype(F32) for j in range(YS)]
    square = sum(jnp.sum(w * w, axis=1, keepdims=True) for w in wide)
    scale = lax.rsqrt(square * (1.0 / D) + 1e-6)
    for q in range(NC):
        part_cols = wide[q // PER_Y][:, (q % PER_Y) * CW:(q % PER_Y + 1) * CW]
        blk[q, 1] = (part_cols * scale * ngain_ref[:, q * CW:(q + 1) * CW]).astype(BF16)
        ag_begin(q)

    def ag_from_left(q, k):
        if k <= HOPS_RIGHT[q]:
            ag["r", q, k].wait_recv()
            if k < HOPS_RIGHT[q]:
                ag_right(q, k + 1)

    def ag_from_right(q, k):
        hops = ZS - 1 - HOPS_RIGHT[q]
        if k <= hops:
            ag["l", q, k].wait_recv()
            if k < hops:
                ag_left(q, k + 1)

    xs = {}

    def select(q, hf):
        source = blk[q, hf * HALF:(hf + 1) * HALF].reshape(HALF * SUB, CW)
        sel[q, hf] = nn(place[hf], source).astype(BF16).reshape(XS * CS, GROUP, CW)
        for j, (dx, dc) in enumerate(PEERS):
            xx, cc = (x + dx) % XS, (c + dc) % CS
            xs[q, hf, j] = go(remote(sel.at[q, hf, xx * CS + cc], xin.at[q, hf, mine_d], xs_send.at[q, hf, j],
                                     xs_recv.at[q, hf, j], seq=seq_id(xx, z, cc)))
        own = pltpu.make_async_copy(sel.at[q, hf, mine_d], xin.at[q, hf, mine_d], loc_sem.at[0, q, hf])
        own.start()
        xs[q, hf, "own"] = own

    def expert_up(q, hf):
        if q == 0 and hf == 0:
            pltpu.make_async_copy(w1, w1, w_sem.at[0]).wait()
        for j in range(len(PEERS)):
            xs[q, hf, j].wait_recv()
        xs[q, hf, "own"].wait()

        def tile(i, _):
            cols = pl.ds(pl.multiple_of((i % 4) * TILE, TILE), TILE)
            value = nn(xin[q, hf].reshape(HROWS, CW), w1[i // 4, q, :, cols])
            if q == 0:
                acc[hf, i] = value
            else:
                acc[hf, i] += value
            return 0

        lax.fori_loop(0, 2 * FF // TILE, tile, 0, unroll=2)

    def activate(hf):
        for n in range(FF // TILE):
            gate = acc[hf, n]
            act[hf, :, n * TILE:(n + 1) * TILE] = (
                gate / (1.0 + jnp.exp(-gate)) * acc[hf, FF // TILE + n]).astype(BF16)

    rt = {}
    order = [(i + (y + 1) * PER_Y) % NC for i in range(NC)]

    def expert_down(i, hf):
        for n in range(CW // TILE):
            cols = pl.ds(n * TILE, TILE)
            value = nn(act[hf], w2[order[i], :, cols]).astype(BF16)
            yout[i, hf, :, :, cols] = value.reshape(XS * CS, GROUP, TILE)

    def send_back(i, hf):
        for j, (dx, dc) in enumerate(PEERS):
            xx, cc = (x + dx) % XS, (c + dc) % CS
            rt[i, hf, j] = go(remote(yout.at[i, hf, xx * CS + cc], ret.at[i, hf, mine_d], rt_send.at[i, hf, j],
                                     rt_recv.at[i, hf, j], seq=seq_id(xx, z, cc)))
        own = pltpu.make_async_copy(yout.at[i, hf, mine_d], ret.at[i, hf, mine_d], loc_sem.at[1, i, hf])
        own.start()
        rt[i, hf, "own"] = own

    for k in range(1, far_k + 1):
        for q in range(NC):
            ag_from_left(q, k)
            ag_from_right(q, k)
            if k == 2:
                select(q, 0)
            if k == far_k:
                select(q, 1)
    for q in range(NC):
        expert_up(q, 0)
    activate(0)
    pltpu.make_async_copy(w2, w2, w_sem.at[1]).wait()
    way_out = list(pending)
    pending.clear()
    for i, hf in PIECES[:EARLY]:
        expert_down(i, hf)
        send_back(i, hf)
    for q in range(NC):
        expert_up(q, 1)
    activate(1)
    for n, (i, hf) in enumerate(PIECES):
        if n >= EARLY:
            expert_down(i, hf)
            if n < WINDOW:
                send_back(i, hf)
    remote(others(state), others(gathered), st_send, st_recv).wait_send()
    remote(others(running), others(prior), pr_send, pr_recv).wait_send()
    for copy in way_out:
        copy.wait_send()

    rs = {}

    def answers(i, hf):
        for j in range(len(PEERS)):
            rt[i, hf, j].wait_recv()
        rt[i, hf, "own"].wait()
        value = ret[i, hf].reshape(HROWS, CW)
        later = PIECES.index((i, hf)) + WINDOW
        if later < len(PIECES):
            send_back(*PIECES[later])
        part[i, hf] = (nn(mixhi[hf], value) + nn(mixlo[hf], value)).reshape(HALF, SUB, CW)

    def own_part(i, k):
        return part[i, at(k) // HALF, at(k) % HALF]

    def gathered_sum(i, k):
        total = own_part(i, k)
        for child, parent in TREES[i].items():
            if parent == k:
                rs[i, child].wait_recv()
                total = total + rs_recv[i, child - 1].astype(F32)
        return total.astype(BF16)

    def pass_on(i, k):
        rs_send[i, k - 1] = gathered_sum(i, k)
        target = seq_id(x, (z + TREES[i][k] - k + ZS) % ZS, c)
        rs[i, k] = go(remote(rs_send.at[i, k - 1], rs_recv.at[i, k - 1], rs_ssem.at[i, k - 1], rs_rsem.at[i, k - 1],
                             seq=target))

    def finish(i):
        total = gathered_sum(i, 0)
        if i < NC - PER_Y:
            mine[i] = total
            peer = (y + 1 + i // PER_Y) % YS
            rs["y", i] = go(remote(mine.at[i], moe.at[y, i % PER_Y], fy_send.at[i], fy_recv.at[i], exp=peer))
        else:
            moe[y, i % PER_Y] = total

    half_time, hop_time = 8.8, 2.8
    spacing = half_time / NC
    events = []
    for i in range(NC):
        near_at = spacing * (PIECES.index((i, 0)) + 1)
        far_at = spacing * (PIECES.index((i, 1)) + 1)
        events.append((near_at, i, 0, functools.partial(answers, i, 0)))
        events.append((far_at, i, 0, functools.partial(answers, i, 1)))
        sent_at = {}

        def ready(k):
            if k not in sent_at:
                held = near_at if k in (7, 0, 1, 2) else far_at
                waits = [ready(child) + hop_time for child, parent in TREES[i].items() if parent == k]
                sent_at[k] = max([held] + waits)
            return sent_at[k]

        for k in range(1, ZS):
            events.append((ready(k), i, 1, functools.partial(pass_on, i, k)))
        events.append((ready(0), i, 2, functools.partial(finish, i)))
    for event in sorted(events, key=lambda event: event[:3]):
        event[3]()

    for i in range(NC - PER_Y):
        rs["y", i].wait_recv()
    for j in range(YS):
        for p in range(PER_Y):
            cols = pl.ds(p * CW, CW)
            sub = pl.ds(j * SUB, SUB)
            out_ref[sub, cols] = (hidden[sub, cols].astype(F32) + moe[j, p].astype(F32)).astype(BF16)

    for copy in pending:
        copy.wait_send()


def per_device(residual, queries, key_vectors, value_vectors, head_gain, norm_gain, routes, route_gates,
               expert_in, expert_out):
    vmem = pl.BlockSpec(memory_space=pltpu.VMEM)
    hbm = pl.BlockSpec(memory_space=pl.ANY)
    dma = pltpu.SemaphoreType.DMA
    peers = len(PEERS)
    return pl.pallas_call(
        layer_kernel,
        out_shape=jax.ShapeDtypeStruct(residual.shape, BF16),
        in_specs=[vmem] * 8 + [hbm] * 2,
        out_specs=vmem,
        scratch_shapes=[
            pltpu.VMEM((2, NC, CW, FF), BF16),
            pltpu.VMEM((NC, FF, CW), BF16),
            pltpu.VMEM((SLAB, PIECE, HEAD), BF16),
            pltpu.VMEM((SLAB, PIECE, HEAD), BF16),
            pltpu.VMEM((SLAB, PIECE, HEAD), BF16),
            pltpu.VMEM((SLAB, PIECE, HEAD), BF16),
            pltpu.VMEM((XS, PIECE, HEAD), F32),
            pltpu.VMEM(residual.shape, F32),
            pltpu.VMEM(residual.shape, BF16),
            pltpu.VMEM((YS, SUB, D // YS), BF16),
            pltpu.VMEM((ZS, SUB, 128), F32),
            pltpu.VMEM((2, HROWS, HALF * SUB), BF16),
            pltpu.VMEM((2, HALF * SUB, HROWS), BF16),
            pltpu.VMEM((2, HALF * SUB, HROWS), BF16),
            pltpu.VMEM((NC, ZS, SUB, CW), BF16),
            pltpu.VMEM((NC, 2, XS * CS, GROUP, CW), BF16),
            pltpu.VMEM((NC, 2, XS * CS, GROUP, CW), BF16),
            pltpu.VMEM((2, 2 * FF // TILE, HROWS, TILE), F32),
            pltpu.VMEM((2, HROWS, FF), BF16),
            pltpu.VMEM((NC, 2, XS * CS, GROUP, CW), BF16),
            pltpu.VMEM((NC, 2, XS * CS, GROUP, CW), BF16),
            pltpu.VMEM((NC, 2, HALF, SUB, CW), F32),
            pltpu.VMEM((NC, ZS - 1, SUB, CW), BF16),
            pltpu.VMEM((NC, ZS - 1, SUB, CW), BF16),
            pltpu.VMEM((NC, SUB, CW), BF16),
            pltpu.VMEM((YS, PER_Y, SUB, CW), BF16),
            dma((2,)), dma, dma, dma((XS - 1,)), dma((XS - 1,)), dma, dma,
            dma((ZS - 1,)), dma((ZS - 1,)),
            dma((YS - 1,)), dma((YS - 1,)),
            dma((NC, ZS - 1)), dma((NC, ZS - 1)),
            dma((NC, 2, peers)), dma((NC, 2, peers)),
            dma((2, NC, 2)),
            dma((NC, 2, peers)), dma((NC, 2, peers)),
            dma((NC, ZS - 1)), dma((NC, ZS - 1)),
            dma((NC,)), dma((NC,)),
        ],
        compiler_params=pltpu.CompilerParams(
            collective_id=0, has_side_effects=True, vmem_limit_bytes=60 * 1024 * 1024),
        name="layer",
    )(queries, key_vectors, value_vectors, residual, head_gain.reshape(1, -1), norm_gain.reshape(1, -1),
      routes.T, route_gates.T, expert_in, expert_out)


def solution(mesh):
    placed = (
        P("seq", "exp"), P("seq", "exp"), P("seq", "exp"), P("seq", "exp"), P("exp"), P(),
        P("seq", None), P("seq", None), P("seq", None, None, None), P("seq", None, None),
    )
    return jax.shard_map(
        per_device, mesh=mesh, in_specs=placed, out_specs=P("seq", "exp"), check_vma=False
    )
```
